512 devices in a mesh: row: 16 (over y_hi, z), col: 32 (over y_lo, x, core).
Axes of the slice: x: 4, y: 8 (y_hi: 2, y_lo: 4; y = y_hi * 4 + y_lo), z: 8, core: 2. Of those that a mesh axis runs over, the one named last changes fastest.
Arguments:
- features: bfloat16 [65536, 256], P(('col', 'row')), may hold values from -6 to 6
- weight: bfloat16 [256, 256], replicated, may hold values from -0.375 to 0.375
- bias: float32 [256], replicated, may hold values from -3 to 3
- grad_out: bfloat16 [65536, 256], P(('row', 'col')), may hold values from -6 to 6
- tile_rows: int32 [16, 32, 128], P('row', 'col'), may hold values from 0 to 31
- tile_cols: int32 [16, 32, 128], P('row', 'col'), may hold values from 0 to 15
- tile_counts: int32 [16, 32], P('row', 'col'), may hold values from 1 to 128, as said below
- tile_values: bfloat16 [16, 32, 128, 128, 128], P('row', 'col'), may hold values from 0 to 0.011962891
Outputs:
- output: bfloat16 [65536, 256], P(('row', 'col'))
- grad_features: bfloat16 [65536, 256], P(('col', 'row'))
- grad_weight: float32 [256, 256], replicated
- grad_bias: float32 [256], replicated
The draws below stay inside these ranges and needn't reach their ends.
Inputs may be any that keep to these rules, and one draw needn't show every extreme that they name: `tile_counts`: some grid cell has all 128 slots live. Tile coordinates may repeat within a cell; repeated tiles add.
All inputs are finite; a program needn't handle non-finite values.
Results may differ from the reference program's by a relative error of at most 0.018.
Values may be sent and summed in bfloat16 or wider, within the bound.
No kernel may reach another device: no remote copies, remote signals or barrier semaphores. Data moves between devices by JAX's collectives and lax.ppermute only.
A program may use at most 64 MiB of HBM per device.

```python
import jax
import jax.numpy as jnp
from jax import lax

C = 256
TILE = 128
SLOTS = 128
VERTICES = 65536
ROW_TILES = 32
COL_TILES = 16
N_ROW = 16
N_COL = 32


def draw_tile_counts(key, part):
    cells = N_ROW * N_COL
    base = jax.random.randint(jax.random.fold_in(key, 11), (cells,), SLOTS // 8, SLOTS // 2 + 1)
    picks = jax.random.randint(jax.random.fold_in(key, 12), (cells,), 0, 16)
    filled = jnp.where(picks == 0, SLOTS, base)
    chosen = jax.random.randint(jax.random.fold_in(key, 13), (), 0, cells)
    filled = jnp.where(jnp.arange(cells) == chosen, SLOTS, filled)
    return filled.reshape(N_ROW, N_COL).astype(jnp.int32)


def plant(values, rng, low, largest):
    shape = values.shape
    index_at = [jax.random.randint(jax.random.fold_in(rng, axis), (), 0, shape[axis]) for axis in range(len(shape))]
    values = values.at[tuple(index_at)].set(low)
    longest = shape.index(max(shape))
    index_at[longest] = (index_at[longest] + 1) % shape[longest]
    return values.at[tuple(index_at)].set(largest)


def block_scale(key, shape, pieces, smallest, top_value):
    gain, own = 1.0, jax.random.fold_in(key, 6)
    for axis_at, parts in pieces:
        steps = jnp.exp(jax.random.uniform(jax.random.fold_in(own, axis_at), (parts,), jnp.float32, smallest / len(pieces), top_value / len(pieces)))
        gain = gain * jnp.repeat(steps, shape[axis_at] // parts).reshape([-1 if axis == axis_at else 1 for axis in range(len(shape))])
    return gain


def gaussian(stream_key, dims, deviation, most, cuts=(), held_as=jnp.bfloat16):
    values = deviation * jax.random.normal(stream_key, dims, jnp.float32)
    if cuts:
        values = values * block_scale(stream_key, dims, cuts, -0.22, 0.18)
    return jnp.clip(values, -most, most).astype(held_as)


def setup_inputs(seed: int = 0) -> dict:
    splits = jax.random.split(jax.random.key(seed), 9)
    features = gaussian(splits[0], (VERTICES, C), 1.0, 6.0, ((0, 512),))
    weight = gaussian(splits[1], (C, C), C ** -0.5, 0.375)
    bias = gaussian(splits[2], (C,), 0.5, 3.0, (), jnp.float32)
    grad_out = gaussian(splits[3], (VERTICES, C), 1.0, 6.0, ((0, 512),))
    tile_rows = plant(jax.random.randint(splits[4], (N_ROW, N_COL, SLOTS), 0, ROW_TILES), jax.random.fold_in(splits[4], 1), 0, ROW_TILES - 1).astype(jnp.int32)
    tile_cols = plant(jax.random.randint(splits[5], (N_ROW, N_COL, SLOTS), 0, COL_TILES), jax.random.fold_in(splits[5], 1), 0, COL_TILES - 1).astype(jnp.int32)
    tile_counts = draw_tile_counts(jax.random.fold_in(splits[8], 71), 0)
    tile_values = jnp.clip(0.011962891 * jax.random.uniform(splits[7], (N_ROW, N_COL, SLOTS, TILE, TILE), jnp.float32) ** block_scale(splits[7], (N_ROW, N_COL, SLOTS, TILE, TILE), ((0, 16), (1, 32)), -0.2, 0.2), 0.0, 0.011962891).astype(jnp.bfloat16)
    return dict(features=features, weight=weight, bias=bias, grad_out=grad_out, tile_rows=tile_rows, tile_cols=tile_cols, tile_counts=tile_counts, tile_values=tile_values)


def elu_value(pre):
    return jnp.where(pre > 0, pre, jnp.expm1(jnp.minimum(pre, 0.0)))


def elu_slope(pre):
    return jnp.where(pre > 0, jnp.float32(1.0), jnp.exp(jnp.minimum(pre, 0.0)))


def cell_terms(values, dest_idx, src_idx, live, source, dest_tiles, transpose):
    blocks = source[src_idx]
    if transpose:
        prod = jnp.einsum("gab,gac->gbc", values.astype(jnp.float32), blocks.astype(jnp.float32))
    else:
        prod = jnp.einsum("gab,gbc->gac", values.astype(jnp.float32), blocks.astype(jnp.float32))
    keep = (jnp.arange(values.shape[0]) < live).astype(jnp.float32)
    onehot = (dest_idx[None, :] == jnp.arange(dest_tiles)[:, None]).astype(jnp.float32) * keep[None, :]
    return jnp.einsum("kg,gac->kac", onehot, prod, precision=lax.Precision.HIGHEST)


def reference(features, weight, bias, grad_out, tile_rows, tile_cols, tile_counts, tile_values):
    mixed = jnp.dot(features, weight, preferred_element_type=jnp.float32).astype(jnp.bfloat16)
    mixed_blocks = mixed.reshape(N_COL, COL_TILES, TILE, C)

    def forward_row(i):
        def add_cell(j, acc):
            return acc + cell_terms(tile_values[i, j], tile_rows[i, j], tile_cols[i, j], tile_counts[i, j], mixed_blocks[j], ROW_TILES, False)
        return lax.fori_loop(0, N_COL, add_cell, jnp.zeros((ROW_TILES, TILE, C), jnp.float32))

    aggregate = lax.map(forward_row, jnp.arange(N_ROW))
    pre = aggregate.reshape(VERTICES, C) + bias[None, :]
    output = elu_value(pre).astype(jnp.bfloat16)
    grad_pre = (grad_out.astype(jnp.float32) * elu_slope(pre)).astype(jnp.bfloat16)
    grad_blocks = grad_pre.reshape(N_ROW, ROW_TILES, TILE, C)

    def backward_col(j):
        def add_cell(i, acc):
            return acc + cell_terms(tile_values[i, j], tile_cols[i, j], tile_rows[i, j], tile_counts[i, j], grad_blocks[i], COL_TILES, True)
        return lax.fori_loop(0, N_ROW, add_cell, jnp.zeros((COL_TILES, TILE, C), jnp.float32))

    grad_mixed = lax.map(backward_col, jnp.arange(N_COL)).reshape(VERTICES, C).astype(jnp.bfloat16)
    grad_features = jnp.dot(grad_mixed, weight.T, preferred_element_type=jnp.float32).astype(jnp.bfloat16)
    grad_weight = jnp.dot(features.T, grad_mixed, preferred_element_type=jnp.float32)
    grad_bias = jnp.sum(grad_pre.astype(jnp.float32), axis=0)
    return (output, grad_features, grad_weight, grad_bias)
```

```python
import functools

import jax
import jax.numpy as jnp
from jax import lax
from jax.experimental import pallas as pl
from jax.experimental.pallas import tpu as pltpu
from jax.sharding import Mesh
from jax.sharding import PartitionSpec as P

ROW = ("yh", "z")
COL = ("yl", "x", "core")
ALL = ROW + COL
CHUNK = 16
GROUP = 4


def elu_value(pre):
    return jnp.where(pre > 0, pre, jnp.expm1(jnp.minimum(pre, 0.0)))


def elu_slope(pre):
    return jnp.where(pre > 0, jnp.float32(1.0), jnp.exp(jnp.minimum(pre, 0.0)))


def col_slot(t):
    return lax.rem(t, 2) * 16 + lax.rem(t // 2, 4) * 4 + t // 8


def start_values(values_hbm, values, sems):
    copies = [
        pltpu.make_async_copy(
            values_hbm.at[pl.ds(c * CHUNK, CHUNK)], values.at[pl.ds(c * CHUNK, CHUNK)], sems.at[c]
        )
        for c in range(values.shape[0] // CHUNK)
    ]
    for copy in copies:
        copy.start()
    return copies


def walk(copies, live, step):
    for c, copy in enumerate(copies):
        copy.wait()
        left = jnp.clip(live - c * CHUNK, 0, CHUNK)

        def one(g, carry, c=c):
            step(c * CHUNK + g * GROUP)
            return carry

        lax.fori_loop(0, (left + GROUP - 1) // GROUP, one, 0)


def forward_kernel(rows, cols, live_ref, values_hbm, src, out, values, acc, sems):
    live = live_ref[0]
    copies = start_values(values_hbm, values, sems)
    tiles = out.shape[0]
    acc[...] = jnp.zeros_like(acc)

    def step(first):
        for u in range(GROUP):
            s = first + u
            dest = jnp.where(s < live, col_slot(rows[s]), tiles)
            acc[dest] += jnp.dot(values[s], src[cols[s]], preferred_element_type=jnp.float32)

    walk(copies, live, step)
    out[...] = acc[:tiles].astype(out.dtype)


def backward_kernel(rows, cols, live_ref, core_ref, values_hbm, own_hbm, other_hbm, out, values, src, acc, sems, src_sems):
    live = live_ref[0]
    core = core_ref[0]
    half = own_hbm.shape[0]
    fetch = [
        pltpu.make_async_copy(own_hbm, src.at[pl.ds(core * half, half)], src_sems.at[0]),
        pltpu.make_async_copy(other_hbm, src.at[pl.ds((1 - core) * half, half)], src_sems.at[1]),
    ]
    for copy in fetch:
        copy.start()
    copies = start_values(values_hbm, values, sems)
    tiles = out.shape[0]
    acc[...] = jnp.zeros_like(acc)
    for copy in fetch:
        copy.wait()

    def step(first):
        for u in range(GROUP):
            s = first + u
            dest = jnp.where(s < live, cols[s], tiles)
            acc[dest] += lax.dot_general(
                values[s],
                src[col_slot(rows[s])],
                (((0,), (0,)), ((), ())),
                preferred_element_type=jnp.float32,
            )

    walk(copies, live, step)
    out[...] = acc[:tiles].astype(out.dtype)


SMEM = pl.BlockSpec(memory_space=pltpu.SMEM)
VMEM = pl.BlockSpec(memory_space=pltpu.VMEM)
ANY = pl.BlockSpec(memory_space=pl.ANY)


def cost(slots, side, width):
    return pl.CostEstimate(
        flops=2 * slots * side * side * width, bytes_accessed=2 * slots * side * side, transcendentals=0
    )


def spread_forward(rows, cols, live, values, src, row_tiles):
    slots, side, _ = values.shape
    width = src.shape[-1]
    return pl.pallas_call(
        forward_kernel,
        out_shape=jax.ShapeDtypeStruct((row_tiles, side, width), jnp.bfloat16),
        in_specs=[SMEM, SMEM, SMEM, ANY, VMEM],
        out_specs=VMEM,
        scratch_shapes=[
            pltpu.VMEM((slots, side, side), jnp.bfloat16),
            pltpu.VMEM((row_tiles + 1, side, width), jnp.float32),
            pltpu.SemaphoreType.DMA((slots // CHUNK,)),
        ],
        compiler_params=pltpu.CompilerParams(vmem_limit_bytes=40 << 20),
        cost_estimate=cost(slots, side, width),
        name="forward_tiles",
    )(rows, cols, live, values, src)


def spread_backward(rows, cols, live, core, values, own, other, col_tiles):
    slots, side, _ = values.shape
    width = own.shape[-1]
    return pl.pallas_call(
        backward_kernel,
        out_shape=jax.ShapeDtypeStruct((col_tiles, side, width), jnp.bfloat16),
        in_specs=[SMEM, SMEM, SMEM, SMEM, ANY, ANY, ANY],
        out_specs=VMEM,
        scratch_shapes=[
            pltpu.VMEM((slots, side, side), jnp.bfloat16),
            pltpu.VMEM((2 * own.shape[0], side, width), jnp.bfloat16),
            pltpu.VMEM((col_tiles + 1, side, width), jnp.float32),
            pltpu.SemaphoreType.DMA((slots // CHUNK,)),
            pltpu.SemaphoreType.DMA((2,)),
        ],
        compiler_params=pltpu.CompilerParams(vmem_limit_bytes=40 << 20),
        cost_estimate=cost(slots, side, width),
        name="backward_tiles",
    )(rows, cols, live, core, values, own, other)


def exchange(x, axes):
    return lax.all_to_all(x, axes, 0, 0, tiled=True)


def gather(x, axes, size):
    copies = lax.optimization_barrier(jnp.broadcast_to(x[None], (size,) + x.shape))
    return exchange(copies, axes)


def add_up(x):
    return jnp.sum(x.astype(jnp.float32), axis=0)


def body(features, weight, bias, grad_out, tile_rows, tile_cols, tile_counts, tile_values):
    values = tile_values[0, 0]
    rows, cols, live = tile_rows[0, 0], tile_cols[0, 0], tile_counts[0]
    side, width = features.shape
    row_tiles, col_tiles = 32, 16
    bf16 = jnp.bfloat16
    core = lax.axis_index("core").astype(jnp.int32).reshape(1)

    block = gather(features, ROW, col_tiles)
    partial = spread_forward(rows, cols, live, values, block, row_tiles)
    by_core = add_up(exchange(partial.reshape(2, 16, side, width), "core")).astype(bf16)
    by_x = add_up(exchange(by_core.reshape(4, 4, side, width), "x")).astype(bf16)
    mean = add_up(exchange(by_x, "yl"))
    pre = (
        jnp.dot(mean, weight.astype(jnp.float32), precision=lax.Precision.HIGHEST, preferred_element_type=jnp.float32)
        + bias[None, :]
    )
    grad_pre = (grad_out.astype(jnp.float32) * elu_slope(pre)).astype(bf16)
    output = elu_value(pre).astype(bf16)

    along_y = gather(grad_pre, "yl", 4)
    own = gather(along_y, "x", 4).reshape(16, side, width)
    other = lax.ppermute(own, "core", [(0, 1), (1, 0)])

    grad32 = grad_pre.astype(jnp.float32)
    weight_term = lax.dot_general(
        mean, grad32, (((0,), (0,)), ((), ())), precision=lax.Precision.HIGHEST, preferred_element_type=jnp.float32
    )
    n = 512
    per = width * width // n
    terms = jnp.concatenate([weight_term.reshape(n, per), jnp.zeros((n, 128), jnp.float32)], axis=1)
    bias_term = jnp.sum(grad32, axis=0).reshape(2, 1, 128)
    terms = terms.at[:, per:].set(jnp.broadcast_to(bias_term, (2, n // 2, 128)).reshape(n, 128))
    piece = add_up(exchange(terms.reshape(n, 1, 2 * per), ALL))
    pieces = gather(piece, ALL, n).reshape(n, 2 * per)
    grad_weight = pieces[:, :per].reshape(width, width)
    grad_bias = jnp.concatenate([pieces[0, per:], pieces[n // 2, per:]])

    back = spread_backward(rows, cols, live, core, values, own, other, col_tiles)
    grad_mixed = add_up(exchange(back, ROW)).astype(bf16)
    grad_features = lax.dot_general(
        grad_mixed, weight, (((1,), (1,)), ((), ())), preferred_element_type=jnp.float32
    ).astype(bf16)
    return (output, grad_features, grad_weight, grad_bias)


def solution(mesh):
    fine = Mesh(mesh.devices.reshape(2, 8, 4, 4, 2), ALL)
    placed = (
        P(COL + ROW, None),
        P(),
        P(),
        P(ALL, None),
        P(ROW, COL, None),
        P(ROW, COL, None),
        P(ROW, COL),
        P(ROW, COL, None, None, None),
    )
    return jax.shard_map(
        body,
        mesh=fine,
        in_specs=placed,
        out_specs=(P(ALL, None), P(COL + ROW, None), P(), P()),
        check_vma=False,
    )
```

```python
import jax
import jax.numpy as jnp
from jax import lax
from jax.experimental import pallas as pl
from jax.experimental.pallas import tpu as pltpu
from jax.sharding import Mesh
from jax.sharding import PartitionSpec as P

ROW = ("yh", "z")
COL = ("yl", "x", "core")
ALL = ROW + COL
CHUNK = 16
GROUP = 4


def elu_value(pre):
    return jnp.where(pre > 0, pre, jnp.expm1(jnp.minimum(pre, 0.0)))


def elu_slope(pre):
    return jnp.where(pre > 0, jnp.float32(1.0), jnp.exp(jnp.minimum(pre, 0.0)))


def col_slot(t):
    return lax.rem(t, 2) * 16 + lax.rem(t // 2, 4) * 4 + t // 8


def start_values(values_hbm, values, sems):
    copies = [
        pltpu.make_async_copy(
            values_hbm.at[pl.ds(c * CHUNK, CHUNK)], values.at[pl.ds(c * CHUNK, CHUNK)], sems.at[c]
        )
        for c in range(values.shape[0] // CHUNK)
    ]
    for copy in copies:
        copy.start()
    return copies


def walk(copies, live, step):
    for c, copy in enumerate(copies):
        copy.wait()
        left = jnp.clip(live - c * CHUNK, 0, CHUNK)

        def one(g, carry, c=c):
            step(c * CHUNK + g * GROUP)
            return carry

        lax.fori_loop(0, (left + GROUP - 1) // GROUP, one, 0)


def forward_kernel(rows, cols, live_ref, values_hbm, src, out, values, acc, sems):
    live = live_ref[0]
    copies = start_values(values_hbm, values, sems)
    tiles = out.shape[0]
    acc[...] = jnp.zeros_like(acc)

    def step(first):
        for u in range(GROUP):
            s = first + u
            dest = jnp.where(s < live, col_slot(rows[s]), tiles)
            acc[dest] += jnp.dot(values[s], src[cols[s]], preferred_element_type=jnp.float32)

    walk(copies, live, step)
    out[...] = acc[:tiles].astype(out.dtype)


def backward_kernel(rows, cols, live_ref, place, values_hbm, *refs):
    blocks, (out, values, src, acc, sems, src_sems) = refs[:8], refs[8:]
    live = live_ref[0]
    core, x = place[0], place[1]
    depth = blocks[0].shape[0]
    fetch = [
        pltpu.make_async_copy(block, src.at[pl.ds(k * depth, depth)], src_sems.at[k]) for k, block in enumerate(blocks)
    ]
    for copy in fetch:
        copy.start()
    copies = start_values(values_hbm, values, sems)
    tiles = out.shape[0]
    acc[...] = jnp.zeros_like(acc)
    for copy in fetch:
        copy.wait()

    def slot(t):
        return (lax.rem(t, 2) ^ core) * 16 + ((x - t // 2) & 3) * 4 + t // 8

    def step(first):
        for u in range(GROUP):
            s = first + u
            dest = jnp.where(s < live, cols[s], tiles)
            acc[dest] += lax.dot_general(
                values[s], src[slot(rows[s])], (((0,), (0,)), ((), ())), preferred_element_type=jnp.float32
            )

    walk(copies, live, step)
    out[...] = acc[:tiles].astype(out.dtype)


def place_kernel(place, pieces, out):
    core, x, y = place[0], place[1], place[2]
    for kc in range(2):
        for kx in range(4):
            for ky in range(4):
                to = ((y - ky) & 3) * 8 + ((x - kx) & 3) * 2 + (core ^ kc)
                out[to] = pieces[kc * 16 + kx * 4 + ky]


SMEM = pl.BlockSpec(memory_space=pltpu.SMEM)
VMEM = pl.BlockSpec(memory_space=pltpu.VMEM)
ANY = pl.BlockSpec(memory_space=pl.ANY)
HBM = pl.BlockSpec(memory_space=pltpu.HBM)


def cost(slots, side, width):
    return pl.CostEstimate(
        flops=2 * slots * side * side * width, bytes_accessed=2 * slots * side * side, transcendentals=0
    )


def spread_forward(rows, cols, live, values, src, row_tiles):
    slots, side, _ = values.shape
    width = src.shape[-1]
    return pl.pallas_call(
        forward_kernel,
        out_shape=jax.ShapeDtypeStruct((row_tiles, side, width), jnp.bfloat16),
        in_specs=[SMEM, SMEM, SMEM, HBM, VMEM],
        out_specs=VMEM,
        scratch_shapes=[
            pltpu.VMEM((slots, side, side), jnp.bfloat16),
            pltpu.VMEM((row_tiles + 1, side, width), jnp.float32),
            pltpu.SemaphoreType.DMA((slots // CHUNK,)),
        ],
        compiler_params=pltpu.CompilerParams(vmem_limit_bytes=40 << 20),
        cost_estimate=cost(slots, side, width),
        name="forward_tiles",
    )(rows, cols, live, values, src)


def spread_backward(rows, cols, live, place, values, blocks, col_tiles):
    slots, side, _ = values.shape
    depth, _, width = blocks[0].shape
    return pl.pallas_call(
        backward_kernel,
        out_shape=jax.ShapeDtypeStruct((col_tiles, side, width), jnp.bfloat16),
        in_specs=[SMEM, SMEM, SMEM, SMEM, HBM] + [ANY] * len(blocks),
        out_specs=VMEM,
        scratch_shapes=[
            pltpu.VMEM((slots, side, side), jnp.bfloat16),
            pltpu.VMEM((len(blocks) * depth, side, width), jnp.bfloat16),
            pltpu.VMEM((col_tiles + 1, side, width), jnp.float32),
            pltpu.SemaphoreType.DMA((slots // CHUNK,)),
            pltpu.SemaphoreType.DMA((len(blocks),)),
        ],
        compiler_params=pltpu.CompilerParams(vmem_limit_bytes=40 << 20),
        cost_estimate=cost(slots, side, width),
        name="backward_tiles",
    )(rows, cols, live, place, values, *blocks)


def put_in_place(place, pieces):
    return pl.pallas_call(
        place_kernel,
        out_shape=jax.ShapeDtypeStruct(pieces.shape, pieces.dtype),
        in_specs=[SMEM, VMEM],
        out_specs=VMEM,
        name="place_pieces",
    )(place, pieces)


def around(x, axis, size):
    return [x] + [lax.ppermute(x, axis, [(i, (i + k) % size) for i in range(size)]) for k in range(1, size)]


def swap(x):
    return lax.ppermute(x, "core", [(0, 1), (1, 0)])


def exchange(x, axes):
    return lax.all_to_all(x, axes, 0, 0, tiled=True)


def gather(x, axes, size):
    copies = lax.optimization_barrier(jnp.broadcast_to(x[None], (size,) + x.shape))
    return exchange(copies, axes)


def add_up(x):
    return jnp.sum(x.astype(jnp.float32), axis=0)


def weight_pieces(weight_term, bias_term, pieces):
    width = bias_term.shape[-1]
    per = weight_term.shape[0] // pieces
    high = bias_term.astype(jnp.bfloat16)
    low = (bias_term - high.astype(jnp.float32)).astype(jnp.bfloat16)
    tail = jnp.concatenate([high[None], low[None], jnp.zeros((per - 2, width), jnp.bfloat16)])
    tail = jnp.broadcast_to(tail[None], (pieces, per, width))
    return jnp.concatenate([weight_term.astype(jnp.bfloat16).reshape(pieces, per, width), tail], axis=1)


def body(features, weight, bias, grad_out, tile_rows, tile_cols, tile_counts, tile_values):
    values = pltpu.with_memory_space_constraint(tile_values[0, 0], pltpu.HBM)
    rows, cols, live = tile_rows[0, 0], tile_cols[0, 0], tile_counts[0]
    side, width = features.shape
    row_tiles, col_tiles = 32, 16
    bf16 = jnp.bfloat16
    place = jnp.stack([lax.axis_index(axis) for axis in ("core", "x", "yl")]).astype(jnp.int32)

    block = gather(features, ROW, col_tiles)
    partial = spread_forward(rows, cols, live, values, block, row_tiles)
    by_core = add_up(exchange(partial.reshape(2, 16, side, width), "core")).astype(bf16)
    by_x = add_up(exchange(by_core.reshape(4, 4, side, width), "x")).astype(bf16)
    mean = add_up(exchange(by_x, "yl"))
    pre = (
        jnp.dot(mean, weight.astype(jnp.float32), precision=lax.Precision.HIGHEST, preferred_element_type=jnp.float32)
        + bias[None, :]
    )
    grad_pre = (grad_out.astype(jnp.float32) * elu_slope(pre)).astype(bf16)
    output = elu_value(pre).astype(bf16)

    grad32 = grad_pre.astype(jnp.float32)
    weight_term = lax.dot_general(
        mean, grad32, (((0,), (0,)), ((), ())), precision=lax.Precision.HIGHEST, preferred_element_type=jnp.float32
    )
    terms = weight_pieces(weight_term, jnp.sum(grad32, axis=0), 32)

    along_y = gather(grad_pre, "yl", 4)
    own = around(along_y, "x", 4)
    other = [swap(block) for block in own]
    of_col = add_up(exchange(terms, COL))
    of_all = add_up(gather(of_col, ROW, 16))
    back = spread_backward(rows, cols, live, place, values, own + other, col_tiles)

    by_y = jnp.stack(around(of_all[:8], "yl", 4))
    by_xy = jnp.concatenate(around(by_y, "x", 4))
    pieces = jnp.concatenate([by_xy, swap(by_xy)])
    grad_weight = put_in_place(place, pieces).reshape(width, width)
    grad_bias = of_all[8] + of_all[9]
    grad_mixed = add_up(exchange(back, ROW)).astype(bf16)
    grad_features = lax.dot_general(
        grad_mixed, weight, (((1,), (1,)), ((), ())), preferred_element_type=jnp.float32
    ).astype(bf16)
    return (output, grad_features, grad_weight, grad_bias)


def solution(mesh):
    fine = Mesh(mesh.devices.reshape(2, 8, 4, 4, 2), ALL)
    placed = (
        P(COL + ROW, None),
        P(),
        P(),
        P(ALL, None),
        P(ROW, COL, None),
        P(ROW, COL, None),
        P(ROW, COL),
        P(ROW, COL, None, None, None),
    )
    return jax.shard_map(
        body,
        mesh=fine,
        in_specs=placed,
        out_specs=(P(ALL, None), P(COL + ROW, None), P(), P()),
        check_vma=False,
    )
```

```python
import jax
import jax.numpy as jnp
from jax import lax
from jax.experimental import pallas as pl
from jax.experimental.pallas import tpu as pltpu
from jax.sharding import Mesh
from jax.sharding import PartitionSpec as P

ROW = ("yh", "z")
COL = ("yl", "x", "core")
ALL = ROW + COL
CHUNK = 16
GROUP = 16


def elu_value(pre):
    return jnp.where(pre > 0, pre, jnp.expm1(jnp.minimum(pre, 0.0)))


def elu_slope(pre):
    return jnp.where(pre > 0, jnp.float32(1.0), jnp.exp(jnp.minimum(pre, 0.0)))


def col_slot(t):
    return lax.rem(t, 2) * 16 + lax.rem(t // 2, 4) * 4 + t // 8


def start_values(values_hbm, values, sems):
    copies = [
        pltpu.make_async_copy(
            values_hbm.at[pl.ds(c * CHUNK, CHUNK)], values.at[pl.ds(c * CHUNK, CHUNK)], sems.at[c]
        )
        for c in range(values.shape[0] // CHUNK)
    ]
    for copy in copies:
        copy.start()
    return copies


def walk(copies, live, step):
    for c, copy in enumerate(copies):
        copy.wait()
        left = jnp.clip(live - c * CHUNK, 0, CHUNK)

        def one(g, carry, c=c):
            step(c * CHUNK + g * GROUP)
            return carry

        lax.fori_loop(0, (left + GROUP - 1) // GROUP, one, 0)


def forward_kernel(rows, cols, live_ref, values_hbm, src, out, values, acc, sems):
    live = live_ref[0]
    copies = start_values(values_hbm, values, sems)
    tiles = out.shape[0]
    acc[...] = jnp.zeros_like(acc)

    def step(first):
        for u in range(GROUP):
            s = first + u
            dest = jnp.where(s < live, col_slot(rows[s]), tiles)
            acc[dest] += jnp.dot(values[s], src[cols[s]], preferred_element_type=jnp.float32)

    walk(copies, live, step)
    out[...] = acc[:tiles].astype(out.dtype)


def backward_kernel(rows, cols, live_ref, place, values_hbm, *refs):
    blocks, (out, values, src, acc, sems, src_sems) = refs[:8], refs[8:]
    live = live_ref[0]
    core, x = place[0], place[1]
    depth = blocks[0].shape[0]
    fetch = [
        pltpu.make_async_copy(block, src.at[pl.ds(k * depth, depth)], src_sems.at[k]) for k, block in enumerate(blocks)
    ]
    for copy in fetch:
        copy.start()
    copies = start_values(values_hbm, values, sems)
    tiles = out.shape[0]
    acc[...] = jnp.zeros_like(acc)
    for copy in fetch:
        copy.wait()

    def slot(t):
        return (lax.rem(t, 2) ^ core) * 16 + ((x - t // 2) & 3) * 4 + t // 8

    def step(first):
        for u in range(GROUP):
            s = first + u
            dest = jnp.where(s < live, cols[s], tiles)
            acc[dest] += lax.dot_general(
                values[s], src[slot(rows[s])], (((0,), (0,)), ((), ())), preferred_element_type=jnp.float32
            )

    walk(copies, live, step)
    out[...] = acc[:tiles].astype(out.dtype)


SMEM = pl.BlockSpec(memory_space=pltpu.SMEM)
VMEM = pl.BlockSpec(memory_space=pltpu.VMEM)
ANY = pl.BlockSpec(memory_space=pl.ANY)
HBM = pl.BlockSpec(memory_space=pltpu.HBM)


def cost(slots, side, width):
    return pl.CostEstimate(
        flops=2 * slots * side * side * width, bytes_accessed=2 * slots * side * side, transcendentals=0
    )


def spread_forward(rows, cols, live, values, src, row_tiles):
    slots, side, _ = values.shape
    width = src.shape[-1]
    return pl.pallas_call(
        forward_kernel,
        out_shape=jax.ShapeDtypeStruct((row_tiles, side, width), jnp.bfloat16),
        in_specs=[SMEM, SMEM, SMEM, HBM, VMEM],
        out_specs=VMEM,
        scratch_shapes=[
            pltpu.VMEM((slots, side, side), jnp.bfloat16),
            pltpu.VMEM((row_tiles + 1, side, width), jnp.float32),
            pltpu.SemaphoreType.DMA((slots // CHUNK,)),
        ],
        compiler_params=pltpu.CompilerParams(vmem_limit_bytes=40 << 20),
        cost_estimate=cost(slots, side, width),
        name="forward_tiles",
    )(rows, cols, live, values, src)


def spread_backward(rows, cols, live, place, values, blocks, col_tiles):
    slots, side, _ = values.shape
    depth, _, width = blocks[0].shape
    return pl.pallas_call(
        backward_kernel,
        out_shape=jax.ShapeDtypeStruct((col_tiles, side, width), jnp.bfloat16),
        in_specs=[SMEM, SMEM, SMEM, SMEM, HBM] + [ANY] * len(blocks),
        out_specs=VMEM,
        scratch_shapes=[
            pltpu.VMEM((slots, side, side), jnp.bfloat16),
            pltpu.VMEM((len(blocks) * depth, side, width), jnp.bfloat16),
            pltpu.VMEM((col_tiles + 1, side, width), jnp.float32),
            pltpu.SemaphoreType.DMA((slots // CHUNK,)),
            pltpu.SemaphoreType.DMA((len(blocks),)),
        ],
        compiler_params=pltpu.CompilerParams(vmem_limit_bytes=40 << 20),
        cost_estimate=cost(slots, side, width),
        name="backward_tiles",
    )(rows, cols, live, place, values, *blocks)


def around(x, axis, size):
    return [x] + [lax.ppermute(x, axis, [(i, (i + k) % size) for i in range(size)]) for k in range(1, size)]


def swap(x):
    return lax.ppermute(x, "core", [(0, 1), (1, 0)])


def exchange(x, axes):
    return lax.all_to_all(x, axes, 0, 0, tiled=True)


def gather(x, axes, size):
    copies = lax.optimization_barrier(jnp.broadcast_to(x[None], (size,) + x.shape))
    return exchange(copies, axes)


def add_up(x):
    return jnp.sum(x.astype(jnp.float32), axis=0)


def weight_pieces(weight_term, bias_term, pieces):
    width = bias_term.shape[-1]
    per = weight_term.shape[0] // pieces
    high = bias_term.astype(jnp.bfloat16)
    low = (bias_term - high.astype(jnp.float32)).astype(jnp.bfloat16)
    tail = jnp.concatenate([high[None], low[None], jnp.zeros((per - 2, width), jnp.bfloat16)])
    tail = jnp.broadcast_to(tail[None], (pieces, per, width))
    return jnp.concatenate([weight_term.astype(jnp.bfloat16).reshape(pieces, per, width), tail], axis=1)


def body(features, weight, bias, grad_out, tile_rows, tile_cols, tile_counts, tile_values):
    values = pltpu.with_memory_space_constraint(tile_values[0, 0], pltpu.HBM)
    rows, cols, live = tile_rows[0, 0], tile_cols[0, 0], tile_counts[0]
    side, width = features.shape
    row_tiles, col_tiles = 32, 16
    bf16 = jnp.bfloat16
    place = jnp.stack([lax.axis_index(axis) for axis in ("core", "x")]).astype(jnp.int32)

    block = gather(features, ROW, col_tiles)
    partial = spread_forward(rows, cols, live, values, block, row_tiles)
    by_core = add_up(exchange(partial.reshape(2, 16, side, width), "core")).astype(bf16)
    by_x = add_up(exchange(by_core.reshape(4, 4, side, width), "x")).astype(bf16)
    mean = add_up(exchange(by_x, "yl"))
    pre = (
        jnp.dot(mean, weight.astype(jnp.float32), precision=lax.Precision.HIGHEST, preferred_element_type=jnp.float32)
        + bias[None, :]
    )
    grad_pre = (grad_out.astype(jnp.float32) * elu_slope(pre)).astype(bf16)
    output = elu_value(pre).astype(bf16)

    grad32 = grad_pre.astype(jnp.float32)
    weight_term = lax.dot_general(
        mean, grad32, (((0,), (0,)), ((), ())), precision=lax.Precision.HIGHEST, preferred_element_type=jnp.float32
    )
    terms = weight_pieces(weight_term, jnp.sum(grad32, axis=0), 32)

    along_y = gather(grad_pre, "yl", 4)
    own = around(along_y, "x", 4)
    other = [swap(block) for block in own]
    of_col = add_up(exchange(terms, COL))
    of_all = add_up(gather(of_col, ROW, 16))
    copies = jnp.broadcast_to(of_all[None, :8], (32, 8, width))
    copies, blocks = lax.optimization_barrier((copies, own + other))
    grad_weight = exchange(copies, COL).reshape(width, width)
    grad_bias = of_all[8] + of_all[9]
    back = spread_backward(rows, cols, live, place, values, blocks, col_tiles)
    grad_mixed = add_up(exchange(back, ROW)).astype(bf16)
    grad_features = lax.dot_general(
        grad_mixed, weight, (((1,), (1,)), ((), ())), preferred_element_type=jnp.float32
    ).astype(bf16)
    return (output, grad_features, grad_weight, grad_bias)


def solution(mesh):
    fine = Mesh(mesh.devices.reshape(2, 8, 4, 4, 2), ALL)
    placed = (
        P(COL + ROW, None),
        P(),
        P(),
        P(ALL, None),
        P(ROW, COL, None),
        P(ROW, COL, None),
        P(ROW, COL),
        P(ROW, COL, None, None, None),
    )
    return jax.shard_map(
        body,
        mesh=fine,
        in_specs=placed,
        out_specs=(P(ALL, None), P(COL + ROW, None), P(), P()),
        check_vma=False,
    )
```

```python
import jax
import jax.numpy as jnp
from jax import lax
from jax.experimental import pallas as pl
from jax.experimental.pallas import tpu as pltpu
from jax.sharding import Mesh
from jax.sharding import PartitionSpec as P

ROW = ("yh", "z")
COL = ("yl", "x", "core")
ALL = ROW + COL
CHUNK = 16
GROUP = 16


def elu_value(pre):
    return jnp.where(pre > 0, pre, jnp.expm1(jnp.minimum(pre, 0.0)))


def elu_slope(pre):
    return jnp.where(pre > 0, jnp.float32(1.0), jnp.exp(jnp.minimum(pre, 0.0)))


def start_values(values_hbm, values, sems):
    copies = [
        pltpu.make_async_copy(
            values_hbm.at[pl.ds(c * CHUNK, CHUNK)], values.at[pl.ds(c * CHUNK, CHUNK)], sems.at[c]
        )
        for c in range(values.shape[0] // CHUNK)
    ]
    for copy in copies:
        copy.start()
    return copies


def walk(copies, live, step):
    for c, copy in enumerate(copies):
        copy.wait()
        left = jnp.clip(live - c * CHUNK, 0, CHUNK)

        def one(g, carry, c=c):
            step(c * CHUNK + g * GROUP)
            return carry

        lax.fori_loop(0, (left + GROUP - 1) // GROUP, one, 0)


def forward_kernel(rows, cols, live_ref, core_ref, values_hbm, src, kept, sent, values, acc, sems):
    live, core = live_ref[0], core_ref[0]
    copies = start_values(values_hbm, values, sems)
    half = kept.shape[0]
    acc[...] = jnp.zeros_like(acc)

    def slot(t):
        return (lax.rem(t, 2) ^ core) * half + ((t // 2) & 3) * 4 + t // 8

    def step(first):
        for u in range(GROUP):
            s = first + u
            dest = jnp.where(s < live, slot(rows[s]), 2 * half)
            acc[dest] += jnp.dot(values[s], src[cols[s]], preferred_element_type=jnp.float32)

    walk(copies, live, step)
    sent[...] = acc[half : 2 * half].astype(sent.dtype)
    kept[...] = acc[:half].astype(kept.dtype)


def backward_kernel(rows, cols, live_ref, core_ref, values_hbm, own, other, out, values, src, acc, sems, src_sems):
    live, core = live_ref[0], core_ref[0]
    fetch = [
        pltpu.make_async_copy(own, src.at[pl.ds(core * 4, 4)], src_sems.at[0]),
        pltpu.make_async_copy(other, src.at[pl.ds((1 - core) * 4, 4)], src_sems.at[1]),
    ]
    for copy in fetch:
        copy.start()
    copies = start_values(values_hbm, values, sems)
    tiles, side = out.shape[0], values.shape[1]
    gathered = 4 * side
    acc[...] = jnp.zeros_like(acc)
    for copy in fetch:
        copy.wait()

    def step(first):
        for u in range(GROUP):
            s = first + u
            dest = jnp.where(s < live, cols[s], tiles)
            t = rows[s]
            block = src[lax.rem(t, 2) * 4 + ((t // 2) & 3), pl.ds(pl.multiple_of(t // 8 * side, side), side), :]
            acc[dest] += lax.dot_general(
                values[s], block, (((0,), (0,)), ((), ())), preferred_element_type=jnp.float32
            )

    walk(copies, live, step)

    terms = jnp.zeros((16, out.shape[-1]), jnp.float32)
    bias = jnp.zeros((8, out.shape[-1]), jnp.float32)
    for k in range(8):
        terms += src[k, gathered:, :].astype(jnp.float32)
        for part in range(0, gathered, side):
            block = src[k, part : part + side, :].astype(jnp.float32)
            bias += jnp.sum(block.reshape(side // 8, 8, -1), axis=0)
    bias = jnp.sum(bias, axis=0, keepdims=True)
    high = bias.astype(jnp.bfloat16).astype(jnp.float32)
    row = lax.broadcasted_iota(jnp.int32, (8, out.shape[-1]), 0)
    tail = jnp.where(row == 0, high, jnp.where(row == 1, bias - high, 0.0))
    mine = jnp.where(core == 0, terms[:8], terms[8:])
    tail = jnp.concatenate([mine, tail]).astype(out.dtype)
    for t in range(tiles):
        out[t, :side, :] = acc[t].astype(out.dtype)
        out[t, side:, :] = tail


SMEM = pl.BlockSpec(memory_space=pltpu.SMEM)
VMEM = pl.BlockSpec(memory_space=pltpu.VMEM)
ANY = pl.BlockSpec(memory_space=pl.ANY)
HBM = pl.BlockSpec(memory_space=pltpu.HBM)


def cost(slots, side, width):
    return pl.CostEstimate(
        flops=2 * slots * side * side * width, bytes_accessed=2 * slots * side * side, transcendentals=0
    )


def spread_forward(rows, cols, live, core, values, src, row_tiles):
    slots, side, _ = values.shape
    width = src.shape[-1]
    half = jax.ShapeDtypeStruct((row_tiles // 2, side, width), jnp.bfloat16)
    return pl.pallas_call(
        forward_kernel,
        out_shape=(half, half),
        in_specs=[SMEM, SMEM, SMEM, SMEM, HBM, VMEM],
        out_specs=(VMEM, VMEM),
        scratch_shapes=[
            pltpu.VMEM((slots, side, side), jnp.bfloat16),
            pltpu.VMEM((row_tiles + 1, side, width), jnp.float32),
            pltpu.SemaphoreType.DMA((slots // CHUNK,)),
        ],
        compiler_params=pltpu.CompilerParams(vmem_limit_bytes=40 << 20),
        cost_estimate=cost(slots, side, width),
        name="forward_tiles",
    )(rows, cols, live, core, values, src)


def spread_backward(rows, cols, live, core, values, own, other, col_tiles):
    slots, side, _ = values.shape
    width = own.shape[-1]
    return pl.pallas_call(
        backward_kernel,
        out_shape=jax.ShapeDtypeStruct((col_tiles, side + 16, width), jnp.bfloat16),
        in_specs=[SMEM, SMEM, SMEM, SMEM, HBM, ANY, ANY],
        out_specs=VMEM,
        scratch_shapes=[
            pltpu.VMEM((slots, side, side), jnp.bfloat16),
            pltpu.VMEM((2 * own.shape[0],) + own.shape[1:], jnp.bfloat16),
            pltpu.VMEM((col_tiles + 1, side, width), jnp.float32),
            pltpu.SemaphoreType.DMA((slots // CHUNK,)),
            pltpu.SemaphoreType.DMA((2,)),
        ],
        compiler_params=pltpu.CompilerParams(vmem_limit_bytes=40 << 20),
        cost_estimate=cost(slots, side, width),
        name="backward_tiles",
    )(rows, cols, live, core, values, own, other)


def swap(x):
    return lax.ppermute(x, "core", [(0, 1), (1, 0)])


def exchange(x, axes):
    return lax.all_to_all(x, axes, 0, 0, tiled=True)


def gather(x, axes, size):
    copies = lax.optimization_barrier(jnp.broadcast_to(x[None], (size,) + x.shape))
    return exchange(copies, axes)


def gather_and_scatter(x, pieces, axes):
    copies = jnp.broadcast_to(x[None], pieces.shape[:1] + x.shape)
    return exchange(lax.optimization_barrier(jnp.concatenate([copies, pieces], axis=1)), axes)


def add_up(x):
    return jnp.sum(x.astype(jnp.float32), axis=0)


def body(features, weight, bias, grad_out, tile_rows, tile_cols, tile_counts, tile_values):
    values = pltpu.with_memory_space_constraint(tile_values[0, 0], pltpu.HBM)
    rows, cols, live = tile_rows[0, 0], tile_cols[0, 0], tile_counts[0]
    side, width = features.shape
    row_tiles, col_tiles = 32, 16
    bf16 = jnp.bfloat16
    core = lax.axis_index("core").astype(jnp.int32).reshape(1)

    block = gather(features, ROW, col_tiles)
    kept, sent = spread_forward(rows, cols, live, core, values, block, row_tiles)
    by_core = (kept.astype(jnp.float32) + swap(sent).astype(jnp.float32)).astype(bf16)
    by_x = add_up(exchange(by_core.reshape(4, 4, side, width), "x")).astype(bf16)
    mean = add_up(exchange(by_x, "yl"))
    pre = (
        jnp.dot(mean, weight.astype(jnp.float32), precision=lax.Precision.HIGHEST, preferred_element_type=jnp.float32)
        + bias[None, :]
    )
    grad_pre = (grad_out.astype(jnp.float32) * elu_slope(pre)).astype(bf16)
    output = elu_value(pre).astype(bf16)

    grad32 = grad_pre.astype(jnp.float32)
    weight_term = lax.dot_general(
        mean, grad32, (((0,), (0,)), ((), ())), precision=lax.Precision.HIGHEST, preferred_element_type=jnp.float32
    )
    terms = weight_term.astype(bf16).reshape(4, width // 4, width)
    along_y = gather_and_scatter(grad_pre, terms, "yl")
    terms = add_up(along_y[:, side:]).astype(bf16).reshape(4, width // 16, width)
    own = gather_and_scatter(along_y[:, :side].reshape(4 * side, width), terms, "x")
    back = spread_backward(rows, cols, live, core, values, own, swap(own), col_tiles)

    reduced = add_up(exchange(back, ROW))
    grad_mixed = reduced[:side].astype(bf16)
    grad_weight = gather(reduced[side : side + 8], COL, 32).reshape(width, width)
    grad_bias = reduced[side + 8] + reduced[side + 9]
    grad_features = lax.dot_general(
        grad_mixed, weight, (((1,), (1,)), ((), ())), preferred_element_type=jnp.float32
    ).astype(bf16)
    return (output, grad_features, grad_weight, grad_bias)


def solution(mesh):
    fine = Mesh(mesh.devices.reshape(2, 8, 4, 4, 2), ALL)
    placed = (
        P(COL + ROW, None),
        P(),
        P(),
        P(ALL, None),
        P(ROW, COL, None),
        P(ROW, COL, None),
        P(ROW, COL),
        P(ROW, COL, None, None, None),
    )
    return jax.shard_map(
        body,
        mesh=fine,
        in_specs=placed,
        out_specs=(P(ALL, None), P(COL + ROW, None), P(), P()),
        check_vma=False,
    )
```

```python
import jax
import jax.numpy as jnp
from jax import lax
from jax.experimental import pallas as pl
from jax.experimental.pallas import tpu as pltpu
from jax.sharding import Mesh
from jax.sharding import PartitionSpec as P

ROW = ("yh", "z")
COL = ("yl", "x", "core")
ALL = ROW + COL
CHUNK = 16
GROUP = 16


def elu_value(pre):
    return jnp.where(pre > 0, pre, jnp.expm1(jnp.minimum(pre, 0.0)))


def elu_slope(pre):
    return jnp.where(pre > 0, jnp.float32(1.0), jnp.exp(jnp.minimum(pre, 0.0)))


def start_values(values_hbm, values, sems):
    copies = [
        pltpu.make_async_copy(
            values_hbm.at[pl.ds(c * CHUNK, CHUNK)], values.at[pl.ds(c * CHUNK, CHUNK)], sems.at[c]
        )
        for c in range(values.shape[0] // CHUNK)
    ]
    for copy in copies:
        copy.start()
    return copies


def walk(copies, live, step):
    for c, copy in enumerate(copies):
        copy.wait()
        left = jnp.clip(live - c * CHUNK, 0, CHUNK)

        def one(g, carry, c=c):
            step(c * CHUNK + g * GROUP)
            return carry

        lax.fori_loop(0, (left + GROUP - 1) // GROUP, one, 0)


def forward_kernel(rows, cols, live_ref, core_ref, values_hbm, src, kept, sent, values, acc, sems):
    live, core = live_ref[0], core_ref[0]
    copies = start_values(values_hbm, values, sems)
    half = kept.shape[0]
    acc[...] = jnp.zeros_like(acc)

    def slot(t):
        return (lax.rem(t, 2) ^ core) * half + ((t // 2) & 3) * 4 + t // 8

    def step(first):
        for u in range(GROUP):
            s = first + u
            dest = jnp.where(s < live, slot(rows[s]), 2 * half)
            acc[dest] += jnp.dot(values[s], src[cols[s]], preferred_element_type=jnp.float32)

    walk(copies, live, step)
    sent[...] = acc[half : 2 * half].astype(sent.dtype)
    kept[...] = acc[:half].astype(kept.dtype)


def backward_kernel(rows, cols, live_ref, place, values_hbm, *refs):
    blocks, (out, values, src, acc, sems, src_sems) = refs[:8], refs[8:]
    live = live_ref[0]
    core, x = place[0], place[1]
    depth = blocks[0].shape[0]
    fetch = [
        pltpu.make_async_copy(block, src.at[pl.ds(k * depth, depth)], src_sems.at[k]) for k, block in enumerate(blocks)
    ]
    for copy in fetch:
        copy.start()
    copies = start_values(values_hbm, values, sems)
    tiles = out.shape[0]
    acc[...] = jnp.zeros_like(acc)
    for copy in fetch:
        copy.wait()

    def slot(t):
        return (lax.rem(t, 2) ^ core) * 16 + ((x - t // 2) & 3) * 4 + t // 8

    def step(first):
        for u in range(GROUP):
            s = first + u
            dest = jnp.where(s < live, cols[s], tiles)
            acc[dest] += lax.dot_general(
                values[s], src[slot(rows[s])], (((0,), (0,)), ((), ())), preferred_element_type=jnp.float32
            )

    walk(copies, live, step)
    out[...] = acc[:tiles].astype(out.dtype)


def place_kernel(place, a, b, c, d, out):
    per = a.shape[0]
    for k, piece in enumerate((a, b, c, d)):
        out[pl.ds(((place[2] - k) & 3) * per, per), :] = piece[...]


SMEM = pl.BlockSpec(memory_space=pltpu.SMEM)
VMEM = pl.BlockSpec(memory_space=pltpu.VMEM)
ANY = pl.BlockSpec(memory_space=pl.ANY)
HBM = pl.BlockSpec(memory_space=pltpu.HBM)


def cost(slots, side, width):
    return pl.CostEstimate(
        flops=2 * slots * side * side * width, bytes_accessed=2 * slots * side * side, transcendentals=0
    )


def spread_forward(rows, cols, live, place, values, src, row_tiles):
    slots, side, _ = values.shape
    width = src.shape[-1]
    half = jax.ShapeDtypeStruct((row_tiles // 2, side, width), jnp.bfloat16)
    return pl.pallas_call(
        forward_kernel,
        out_shape=(half, half),
        in_specs=[SMEM, SMEM, SMEM, SMEM, HBM, VMEM],
        out_specs=(VMEM, VMEM),
        scratch_shapes=[
            pltpu.VMEM((slots, side, side), jnp.bfloat16),
            pltpu.VMEM((row_tiles + 1, side, width), jnp.float32),
            pltpu.SemaphoreType.DMA((slots // CHUNK,)),
        ],
        compiler_params=pltpu.CompilerParams(vmem_limit_bytes=40 << 20),
        cost_estimate=cost(slots, side, width),
        name="forward_tiles",
    )(rows, cols, live, place, values, src)


def spread_backward(rows, cols, live, place, values, blocks, col_tiles):
    slots, side, _ = values.shape
    depth, _, width = blocks[0].shape
    return pl.pallas_call(
        backward_kernel,
        out_shape=jax.ShapeDtypeStruct((col_tiles, side, width), jnp.bfloat16),
        in_specs=[SMEM, SMEM, SMEM, SMEM, HBM] + [ANY] * len(blocks),
        out_specs=VMEM,
        scratch_shapes=[
            pltpu.VMEM((slots, side, side), jnp.bfloat16),
            pltpu.VMEM((len(blocks) * depth, side, width), jnp.bfloat16),
            pltpu.VMEM((col_tiles + 1, side, width), jnp.float32),
            pltpu.SemaphoreType.DMA((slots // CHUNK,)),
            pltpu.SemaphoreType.DMA((len(blocks),)),
        ],
        compiler_params=pltpu.CompilerParams(vmem_limit_bytes=40 << 20),
        cost_estimate=cost(slots, side, width),
        name="backward_tiles",
    )(rows, cols, live, place, values, *blocks)


def put_in_place(place, pieces):
    per, width = pieces[0].shape
    return pl.pallas_call(
        place_kernel,
        out_shape=jax.ShapeDtypeStruct((len(pieces) * per, width), pieces[0].dtype),
        in_specs=[SMEM] + [VMEM] * len(pieces),
        out_specs=VMEM,
        name="place_pieces",
    )(place, *pieces)


def around(x, axis, size):
    return [x] + [lax.ppermute(x, axis, [(i, (i + k) % size) for i in range(size)]) for k in range(1, size)]


def swap(x):
    return lax.ppermute(x, "core", [(0, 1), (1, 0)])


def exchange(x, axes):
    return lax.all_to_all(x, axes, 0, 0, tiled=True)


def gather(x, axes, size):
    copies = lax.optimization_barrier(jnp.broadcast_to(x[None], (size,) + x.shape))
    return exchange(copies, axes)


def gather_and_scatter(x, pieces, axes):
    copies = jnp.broadcast_to(x[None], pieces.shape[:1] + x.shape)
    return exchange(lax.optimization_barrier(jnp.concatenate([copies, pieces], axis=1)), axes)


def add_up(x):
    return jnp.sum(x.astype(jnp.float32), axis=0)


def two_rows(x):
    high = x.astype(jnp.bfloat16).astype(jnp.float32)
    row = lax.broadcasted_iota(jnp.int32, (8, x.shape[-1]), 0)
    return jnp.where(row == 0, high, jnp.where(row == 1, x - high, 0.0)).astype(jnp.bfloat16)


def body(features, weight, bias, grad_out, tile_rows, tile_cols, tile_counts, tile_values):
    values = pltpu.with_memory_space_constraint(tile_values[0, 0], pltpu.HBM)
    rows, cols, live = tile_rows[0, 0], tile_cols[0, 0], tile_counts[0]
    side, width = features.shape
    row_tiles, col_tiles = 32, 16
    bf16 = jnp.bfloat16
    place = jnp.stack([lax.axis_index(axis) for axis in ("core", "x", "yl")]).astype(jnp.int32)

    block = gather(features, ROW, col_tiles)
    kept, sent = spread_forward(rows, cols, live, place, values, block, row_tiles)
    by_core = (kept.astype(jnp.float32) + swap(sent).astype(jnp.float32)).astype(bf16)
    by_x = add_up(exchange(by_core.reshape(4, 4, side, width), "x")).astype(bf16)
    mean = add_up(exchange(by_x, "yl"))
    pre = (
        jnp.dot(mean, weight.astype(jnp.float32), precision=lax.Precision.HIGHEST, preferred_element_type=jnp.float32)
        + bias[None, :]
    )
    grad_pre = (grad_out.astype(jnp.float32) * elu_slope(pre)).astype(bf16)
    output = elu_value(pre).astype(bf16)

    grad32 = grad_pre.astype(jnp.float32)
    weight_term = lax.dot_general(
        mean, grad32, (((0,), (0,)), ((), ())), precision=lax.Precision.HIGHEST, preferred_element_type=jnp.float32
    )
    bias_term = jnp.sum(grad32, axis=0, keepdims=True)
    terms = weight_term.astype(bf16).reshape(4, width // 4, width)
    tail = jnp.broadcast_to(two_rows(bias_term)[None], (4, 8, width))
    along_y = gather_and_scatter(grad_pre, jnp.concatenate([terms, tail], axis=1), "yl")

    own = around(along_y[:, :side], "x", 4)
    blocks = own + [swap(block) for block in own]
    terms = add_up(along_y[:, side:])
    rows_of_weight = width // 4
    terms = jnp.concatenate(
        [
            terms[:rows_of_weight].astype(bf16),
            two_rows(terms[rows_of_weight : rows_of_weight + 1] + terms[rows_of_weight + 1 : rows_of_weight + 2]),
        ]
    )
    terms = add_up(gather(terms, ROW, 16))
    back = spread_backward(rows, cols, live, place, values, blocks, col_tiles)
    grad_mixed = add_up(exchange(back, ROW)).astype(bf16)

    terms = terms + swap(terms)
    for bit in (1, 2):
        terms = terms + lax.ppermute(terms, "x", [(i, i ^ bit) for i in range(4)])
    grad_bias = terms[rows_of_weight] + terms[rows_of_weight + 1]
    grad_weight = put_in_place(place, around(terms[:rows_of_weight], "yl", 4))
    grad_features = lax.dot_general(
        grad_mixed, weight, (((1,), (1,)), ((), ())), preferred_element_type=jnp.float32
    ).astype(bf16)
    return (output, grad_features, grad_weight, grad_bias)


def solution(mesh):
    fine = Mesh(mesh.devices.reshape(2, 8, 4, 4, 2), ALL)
    placed = (
        P(COL + ROW, None),
        P(),
        P(),
        P(ALL, None),
        P(ROW, COL, None),
        P(ROW, COL, None),
        P(ROW, COL),
        P(ROW, COL, None, None, None),
    )
    return jax.shard_map(
        body,
        mesh=fine,
        in_specs=placed,
        out_specs=(P(ALL, None), P(COL + ROW, None), P(), P()),
        check_vma=False,
    )
```

```python
import jax
import jax.numpy as jnp
from jax import lax
from jax.experimental import pallas as pl
from jax.experimental.pallas import tpu as pltpu
from jax.sharding import Mesh
from jax.sharding import PartitionSpec as P

ROW = ("yh", "z")
COL = ("yl", "x", "core")
ALL = ROW + COL
CHUNK = 16
GROUP = 16


def elu_value(pre):
    return jnp.where(pre > 0, pre, jnp.expm1(jnp.minimum(pre, 0.0)))


def elu_slope(pre):
    return jnp.where(pre > 0, jnp.float32(1.0), jnp.exp(jnp.minimum(pre, 0.0)))


def start_values(values_hbm, values, sems):
    copies = [
        pltpu.make_async_copy(
            values_hbm.at[pl.ds(c * CHUNK, CHUNK)], values.at[pl.ds(c * CHUNK, CHUNK)], sems.at[c]
        )
        for c in range(values.shape[0] // CHUNK)
    ]
    for copy in copies:
        copy.start()
    return copies


def walk(copies, live, step):
    for c, copy in enumerate(copies):
        copy.wait()
        left = jnp.clip(live - c * CHUNK, 0, CHUNK)

        def one(g, carry, c=c):
            step(c * CHUNK + g * GROUP)
            return carry

        lax.fori_loop(0, (left + GROUP - 1) // GROUP, one, 0)


def forward_kernel(rows, cols, live_ref, core_ref, values_hbm, src, kept, sent, values, acc, sems):
    live, core = live_ref[0], core_ref[0]
    copies = start_values(values_hbm, values, sems)
    half = kept.shape[0]
    acc[...] = jnp.zeros_like(acc)

    def slot(t):
        return (lax.rem(t, 2) ^ core) * half + ((t // 2) & 3) * 4 + t // 8

    def step(first):
        for u in range(GROUP):
            s = first + u
            dest = jnp.where(s < live, slot(rows[s]), 2 * half)
            acc[dest] += jnp.dot(values[s], src[cols[s]], preferred_element_type=jnp.float32)

    walk(copies, live, step)
    sent[...] = acc[half : 2 * half].astype(sent.dtype)
    kept[...] = acc[:half].astype(kept.dtype)


def backward_kernel(rows, cols, live_ref, core_ref, values_hbm, own, other, out, values, src, acc, sems, src_sems):
    live, core = live_ref[0], core_ref[0]
    fetch = [
        pltpu.make_async_copy(own, src.at[pl.ds(core * 4, 4)], src_sems.at[0]),
        pltpu.make_async_copy(other, src.at[pl.ds((1 - core) * 4, 4)], src_sems.at[1]),
    ]
    for copy in fetch:
        copy.start()
    copies = start_values(values_hbm, values, sems)
    tiles, side = out.shape[0], values.shape[1]
    gathered = 4 * side
    acc[...] = jnp.zeros_like(acc)
    for copy in fetch:
        copy.wait()

    def step(first):
        for u in range(GROUP):
            s = first + u
            dest = jnp.where(s < live, cols[s], tiles)
            t = rows[s]
            block = src[lax.rem(t, 2) * 4 + ((t // 2) & 3), pl.ds(pl.multiple_of(t // 8 * side, side), side), :]
            acc[dest] += lax.dot_general(
                values[s], block, (((0,), (0,)), ((), ())), preferred_element_type=jnp.float32
            )

    walk(copies, live, step)

    terms = jnp.zeros((16, out.shape[-1]), jnp.float32)
    bias = jnp.zeros((8, out.shape[-1]), jnp.float32)
    for k in range(8):
        terms += src[k, gathered:, :].astype(jnp.float32)
        for part in range(0, gathered, side):
            block = src[k, part : part + side, :].astype(jnp.float32)
            bias += jnp.sum(block.reshape(side // 8, 8, -1), axis=0)
    bias = jnp.sum(bias, axis=0, keepdims=True)
    high = bias.astype(jnp.bfloat16).astype(jnp.float32)
    row = lax.broadcasted_iota(jnp.int32, (8, out.shape[-1]), 0)
    tail = jnp.where(row == 0, high, jnp.where(row == 1, bias - high, 0.0))
    mine = jnp.where(core == 0, terms[:8], terms[8:])
    tail = jnp.concatenate([mine, tail]).astype(out.dtype)
    for t in range(tiles):
        out[t, :side, :] = acc[t].astype(out.dtype)
        out[t, side:, :] = tail


SMEM = pl.BlockSpec(memory_space=pltpu.SMEM)
VMEM = pl.BlockSpec(memory_space=pltpu.VMEM)
ANY = pl.BlockSpec(memory_space=pl.ANY)
HBM = pl.BlockSpec(memory_space=pltpu.HBM)


def cost(slots, side, width):
    return pl.CostEstimate(
        flops=2 * slots * side * side * width, bytes_accessed=2 * slots * side * side, transcendentals=0
    )


def spread_forward(rows, cols, live, core, values, src, row_tiles):
    slots, side, _ = values.shape
    width = src.shape[-1]
    half = jax.ShapeDtypeStruct((row_tiles // 2, side, width), jnp.bfloat16)
    return pl.pallas_call(
        forward_kernel,
        out_shape=(half, half),
        in_specs=[SMEM, SMEM, SMEM, SMEM, HBM, VMEM],
        out_specs=(VMEM, VMEM),
        scratch_shapes=[
            pltpu.VMEM((slots, side, side), jnp.bfloat16),
            pltpu.VMEM((row_tiles + 1, side, width), jnp.float32),
            pltpu.SemaphoreType.DMA((slots // CHUNK,)),
        ],
        compiler_params=pltpu.CompilerParams(vmem_limit_bytes=40 << 20),
        cost_estimate=cost(slots, side, width),
        name="forward_tiles",
    )(rows, cols, live, core, values, src)


def spread_backward(rows, cols, live, core, values, own, other, col_tiles):
    slots, side, _ = values.shape
    width = own.shape[-1]
    return pl.pallas_call(
        backward_kernel,
        out_shape=jax.ShapeDtypeStruct((col_tiles, side + 16, width), jnp.bfloat16),
        in_specs=[SMEM, SMEM, SMEM, SMEM, HBM, ANY, ANY],
        out_specs=VMEM,
        scratch_shapes=[
            pltpu.VMEM((slots, side, side), jnp.bfloat16),
            pltpu.VMEM((2 * own.shape[0],) + own.shape[1:], jnp.bfloat16),
            pltpu.VMEM((col_tiles + 1, side, width), jnp.float32),
            pltpu.SemaphoreType.DMA((slots // CHUNK,)),
            pltpu.SemaphoreType.DMA((2,)),
        ],
        compiler_params=pltpu.CompilerParams(vmem_limit_bytes=40 << 20),
        cost_estimate=cost(slots, side, width),
        name="backward_tiles",
    )(rows, cols, live, core, values, own, other)


def swap(x):
    return lax.ppermute(x, "core", [(0, 1), (1, 0)])


def exchange(x, axes):
    return lax.all_to_all(x, axes, 0, 0, tiled=True)


def gather(x, axes, size):
    copies = lax.optimization_barrier(jnp.broadcast_to(x[None], (size,) + x.shape))
    return exchange(copies, axes)


def gather_and_scatter(x, pieces, axes):
    copies = jnp.broadcast_to(x[None], pieces.shape[:1] + x.shape)
    return exchange(lax.optimization_barrier(jnp.concatenate([copies, pieces], axis=1)), axes)


def add_up(x):
    return jnp.sum(x.astype(jnp.float32), axis=0)


def body(features, weight, bias, grad_out, tile_rows, tile_cols, tile_counts, tile_values):
    values = pltpu.with_memory_space_constraint(tile_values[0, 0], pltpu.HBM)
    rows, cols, live = tile_rows[0, 0], tile_cols[0, 0], tile_counts[0]
    side, width = features.shape
    row_tiles, col_tiles = 32, 16
    bf16 = jnp.bfloat16
    core = lax.axis_index("core").astype(jnp.int32).reshape(1)
    line = lax.axis_index("yl")
    around = [grad_out] + [lax.ppermute(grad_out, "yl", [(i, (i + k) % 4) for i in range(4)]) for k in range(1, 4)]
    grad_line = jnp.stack([lax.select_n((line - t) & 3, *around) for t in range(4)])

    block, grad_line = lax.optimization_barrier((gather(features, ROW, col_tiles), grad_line))
    kept, sent = spread_forward(rows, cols, live, core, values, block, row_tiles)
    by_core = (kept.astype(jnp.float32) + swap(sent).astype(jnp.float32)).astype(bf16)
    by_x = add_up(exchange(by_core.reshape(4, 4, side, width), "x")).astype(bf16)
    mean = add_up(gather(by_x, "yl", 4)).reshape(4 * side, width)
    pre = (
        jnp.dot(mean, weight.astype(jnp.float32), precision=lax.Precision.HIGHEST, preferred_element_type=jnp.float32)
        + bias[None, :]
    )
    grad_pre = (grad_line.reshape(4 * side, width).astype(jnp.float32) * elu_slope(pre)).astype(bf16)
    output = elu_value(lax.dynamic_slice_in_dim(pre, line * side, side, 0)).astype(bf16)

    mine = lax.dynamic_slice_in_dim(mean, line * (width // 4), width // 4, 1)
    weight_term = lax.dot_general(
        mine,
        grad_pre.astype(jnp.float32),
        (((0,), (0,)), ((), ())),
        precision=lax.Precision.HIGHEST,
        preferred_element_type=jnp.float32,
    )
    terms = weight_term.astype(bf16).reshape(4, width // 16, width)
    own = gather_and_scatter(grad_pre, terms, "x")
    back = spread_backward(rows, cols, live, core, values, own, swap(own), col_tiles)

    reduced = add_up(exchange(back, ROW))
    grad_mixed = reduced[:side].astype(bf16)
    grad_weight = gather(reduced[side : side + 8], COL, 32).reshape(width, width)
    grad_bias = reduced[side + 8] + reduced[side + 9]
    grad_features = lax.dot_general(
        grad_mixed, weight, (((1,), (1,)), ((), ())), preferred_element_type=jnp.float32
    ).astype(bf16)
    return (output, grad_features, grad_weight, grad_bias)


def solution(mesh):
    fine = Mesh(mesh.devices.reshape(2, 8, 4, 4, 2), ALL)
    placed = (
        P(COL + ROW, None),
        P(),
        P(),
        P(ALL, None),
        P(ROW, COL, None),
        P(ROW, COL, None),
        P(ROW, COL),
        P(ROW, COL, None, None, None),
    )
    return jax.shard_map(
        body,
        mesh=fine,
        in_specs=placed,
        out_specs=(P(ALL, None), P(COL + ROW, None), P(), P()),
        check_vma=False,
    )
```

```python
import jax
import jax.numpy as jnp
from jax import lax
from jax.experimental import pallas as pl
from jax.experimental.pallas import tpu as pltpu
from jax.sharding import Mesh
from jax.sharding import PartitionSpec as P

ROW = ("yh", "z")
COL = ("yl", "x", "core")
ALL = ROW + COL
CHUNK = 16
GROUP = 16


def elu_value(pre):
    return jnp.where(pre > 0, pre, jnp.expm1(jnp.minimum(pre, 0.0)))


def elu_slope(pre):
    return jnp.where(pre > 0, jnp.float32(1.0), jnp.exp(jnp.minimum(pre, 0.0)))


def start_values(values_hbm, values, sems):
    copies = [
        pltpu.make_async_copy(
            values_hbm.at[pl.ds(c * CHUNK, CHUNK)], values.at[pl.ds(c * CHUNK, CHUNK)], sems.at[c]
        )
        for c in range(values.shape[0] // CHUNK)
    ]
    for copy in copies:
        copy.start()
    return copies


def walk(copies, live, step):
    for c, copy in enumerate(copies):
        copy.wait()
        left = jnp.clip(live - c * CHUNK, 0, CHUNK)

        def one(g, carry, c=c):
            step(c * CHUNK + g * GROUP)
            return carry

        lax.fori_loop(0, (left + GROUP - 1) // GROUP, one, 0)


def pair_slot(t, half):
    return (t & 7) * 2 + (t // 8 ^ half)


def forward_kernel(rows, cols, live_ref, place, values_hbm, src, kept, sent, values, acc, sems):
    live, core, yh = live_ref[0], place[0], place[1]
    copies = start_values(values_hbm, values, sems)
    half = kept.shape[0]
    acc[...] = jnp.zeros_like(acc)

    def slot(t):
        return (lax.rem(t, 2) ^ core) * half + ((t // 2) & 3) * 4 + t // 8

    def step(first):
        for u in range(GROUP):
            s = first + u
            dest = jnp.where(s < live, slot(rows[s]), 2 * half)
            acc[dest] += jnp.dot(values[s], src[pair_slot(cols[s], yh)], preferred_element_type=jnp.float32)

    walk(copies, live, step)
    sent[...] = acc[half : 2 * half].astype(sent.dtype)
    kept[...] = acc[:half].astype(kept.dtype)


def backward_kernel(rows, cols, live_ref, place, values_hbm, own, other, out, values, src, acc, sems, src_sems):
    live, core, yh = live_ref[0], place[0], place[1]
    fetch = [
        pltpu.make_async_copy(own, src.at[pl.ds(core * 4, 4)], src_sems.at[0]),
        pltpu.make_async_copy(other, src.at[pl.ds((1 - core) * 4, 4)], src_sems.at[1]),
    ]
    for copy in fetch:
        copy.start()
    copies = start_values(values_hbm, values, sems)
    side = values.shape[1]
    tiles = acc.shape[0] - 1
    gathered = 4 * side
    acc[...] = jnp.zeros_like(acc)
    for copy in fetch:
        copy.wait()

    terms = jnp.zeros((16, out.shape[-1]), jnp.float32)
    bias = jnp.zeros((8, out.shape[-1]), jnp.float32)
    for k in range(8):
        terms += src[k, gathered:, :].astype(jnp.float32)
        for part in range(0, gathered, side):
            block = src[k, part : part + side, :].astype(jnp.float32)
            bias += jnp.sum(block.reshape(side // 8, 8, -1), axis=0)
    bias = jnp.sum(bias, axis=0, keepdims=True)
    high = bias.astype(jnp.bfloat16).astype(jnp.float32)
    row = lax.broadcasted_iota(jnp.int32, (8, out.shape[-1]), 0)
    tail = jnp.where(row == 0, high, jnp.where(row == 1, bias - high, 0.0))
    mine = jnp.where(core == 0, terms[:8], terms[8:])
    tail = jnp.concatenate([mine, tail]).astype(out.dtype)
    for z in range(out.shape[0]):
        out[z, 2 * side :, :] = tail

    def step(first):
        for u in range(GROUP):
            s = first + u
            dest = jnp.where(s < live, pair_slot(cols[s], yh), tiles)
            t = rows[s]
            block = src[lax.rem(t, 2) * 4 + ((t // 2) & 3), pl.ds(pl.multiple_of(t // 8 * side, side), side), :]
            acc[dest] += lax.dot_general(
                values[s], block, (((0,), (0,)), ((), ())), preferred_element_type=jnp.float32
            )

    walk(copies, live, step)
    for z in range(out.shape[0]):
        out[z, :side, :] = acc[2 * z].astype(out.dtype)
        out[z, side : 2 * side, :] = acc[2 * z + 1].astype(out.dtype)


SMEM = pl.BlockSpec(memory_space=pltpu.SMEM)
VMEM = pl.BlockSpec(memory_space=pltpu.VMEM)
ANY = pl.BlockSpec(memory_space=pl.ANY)
HBM = pl.BlockSpec(memory_space=pltpu.HBM)


def cost(slots, side, width):
    return pl.CostEstimate(
        flops=2 * slots * side * side * width, bytes_accessed=2 * slots * side * side, transcendentals=0
    )


def spread_forward(rows, cols, live, place, values, src, row_tiles):
    slots, side, _ = values.shape
    width = src.shape[-1]
    half = jax.ShapeDtypeStruct((row_tiles // 2, side, width), jnp.bfloat16)
    return pl.pallas_call(
        forward_kernel,
        out_shape=(half, half),
        in_specs=[SMEM, SMEM, SMEM, SMEM, HBM, VMEM],
        out_specs=(VMEM, VMEM),
        scratch_shapes=[
            pltpu.VMEM((slots, side, side), jnp.bfloat16),
            pltpu.VMEM((row_tiles + 1, side, width), jnp.float32),
            pltpu.SemaphoreType.DMA((slots // CHUNK,)),
        ],
        compiler_params=pltpu.CompilerParams(vmem_limit_bytes=40 << 20),
        cost_estimate=cost(slots, side, width),
        name="forward_tiles",
    )(rows, cols, live, place, values, src)


def spread_backward(rows, cols, live, place, values, own, other, col_tiles):
    slots, side, _ = values.shape
    width = own.shape[-1]
    return pl.pallas_call(
        backward_kernel,
        out_shape=jax.ShapeDtypeStruct((col_tiles // 2, 2 * side + 16, width), jnp.bfloat16),
        in_specs=[SMEM, SMEM, SMEM, SMEM, HBM, ANY, ANY],
        out_specs=VMEM,
        scratch_shapes=[
            pltpu.VMEM((slots, side, side), jnp.bfloat16),
            pltpu.VMEM((2 * own.shape[0],) + own.shape[1:], jnp.bfloat16),
            pltpu.VMEM((col_tiles + 1, side, width), jnp.float32),
            pltpu.SemaphoreType.DMA((slots // CHUNK,)),
            pltpu.SemaphoreType.DMA((2,)),
        ],
        compiler_params=pltpu.CompilerParams(vmem_limit_bytes=40 << 20),
        cost_estimate=cost(slots, side, width),
        name="backward_tiles",
    )(rows, cols, live, place, values, own, other)


def swap(x):
    return lax.ppermute(x, "core", [(0, 1), (1, 0)])


def exchange(x, axes):
    return lax.all_to_all(x, axes, 0, 0, tiled=True)


def gather(x, axes, size):
    copies = lax.optimization_barrier(jnp.broadcast_to(x[None], (size,) + x.shape))
    return exchange(copies, axes)


def gather_and_scatter(x, pieces, axes):
    copies = jnp.broadcast_to(x[None], pieces.shape[:1] + x.shape)
    return exchange(lax.optimization_barrier(jnp.concatenate([copies, pieces], axis=1)), axes)


def add_up(x):
    return jnp.sum(x.astype(jnp.float32), axis=0)


def in_two(x):
    high = lax.reduce_precision(x, 8, 7)
    return jnp.concatenate([high, lax.reduce_precision(x - high, 8, 7)])


def body(features, weight, bias, grad_out, tile_rows, tile_cols, tile_counts, tile_values):
    values = pltpu.with_memory_space_constraint(tile_values[0, 0], pltpu.HBM)
    rows, cols, live = tile_rows[0, 0], tile_cols[0, 0], tile_counts[0]
    side, width = features.shape
    row_tiles, col_tiles = 32, 16
    bf16 = jnp.bfloat16
    place = jnp.stack([lax.axis_index(axis) for axis in ("core", "yh")]).astype(jnp.int32)

    pair = jnp.stack([features, lax.ppermute(features, "yh", [(0, 1), (1, 0)])])
    block = gather(pair, "z", 8).reshape(col_tiles, side, width)
    kept, sent = spread_forward(rows, cols, live, place, values, block, row_tiles)
    by_core = (kept.astype(jnp.float32) + swap(sent).astype(jnp.float32)).astype(bf16)
    by_x = add_up(exchange(by_core.reshape(4, 4, side, width), "x")).astype(bf16)
    mean = add_up(exchange(by_x, "yl"))
    pre = (
        jnp.dot(mean, weight.astype(jnp.float32), precision=lax.Precision.HIGHEST, preferred_element_type=jnp.float32)
        + bias[None, :]
    )
    grad_pre = (grad_out.astype(jnp.float32) * elu_slope(pre)).astype(bf16)
    output = elu_value(pre).astype(bf16)

    grad32 = grad_pre.astype(jnp.float32)
    weight_term = lax.dot_general(
        mean, grad32, (((0,), (0,)), ((), ())), precision=lax.Precision.HIGHEST, preferred_element_type=jnp.float32
    )
    terms = weight_term.astype(bf16).reshape(4, width // 4, width)
    along_y = gather_and_scatter(grad_pre, terms, "yl")
    terms = add_up(along_y[:, side:]).astype(bf16).reshape(4, width // 16, width)
    own = gather_and_scatter(along_y[:, :side].reshape(4 * side, width), terms, "x")
    back = spread_backward(rows, cols, live, place, values, own, swap(own), col_tiles)

    reduced = add_up(exchange(back, "z"))
    mine = in_two(reduced[2 * side :])
    sent = jnp.concatenate([reduced[side : 2 * side].astype(bf16), mine.astype(bf16)])
    sent = lax.ppermute(sent, "yh", [(0, 1), (1, 0)]).astype(jnp.float32)
    grad_mixed = (reduced[:side] + sent[:side]).astype(bf16)
    theirs = sent[side:]
    total = (mine[:16] + mine[16:]) + (theirs[:16] + theirs[16:])
    grad_weight = gather(total[:8], COL, 32).reshape(width, width)
    grad_bias = total[8] + total[9]
    grad_features = lax.dot_general(
        grad_mixed, weight, (((1,), (1,)), ((), ())), preferred_element_type=jnp.float32
    ).astype(bf16)
    return (output, grad_features, grad_weight, grad_bias)


def solution(mesh):
    fine = Mesh(mesh.devices.reshape(2, 8, 4, 4, 2), ALL)
    placed = (
        P(COL + ROW, None),
        P(),
        P(),
        P(ALL, None),
        P(ROW, COL, None),
        P(ROW, COL, None),
        P(ROW, COL),
        P(ROW, COL, None, None, None),
    )
    return jax.shard_map(
        body,
        mesh=fine,
        in_specs=placed,
        out_specs=(P(ALL, None), P(COL + ROW, None), P(), P()),
        check_vma=False,
    )
```

```python
import jax
import jax.numpy as jnp
from jax import lax
from jax.experimental import pallas as pl
from jax.experimental.pallas import tpu as pltpu
from jax.sharding import Mesh
from jax.sharding import PartitionSpec as P

ROW = ("yh", "z")
COL = ("yl", "x", "core")
ALL = ROW + COL
CHUNK = 16
GROUP = 16


def elu_value(pre):
    return jnp.where(pre > 0, pre, jnp.expm1(jnp.minimum(pre, 0.0)))


def elu_slope(pre):
    return jnp.where(pre > 0, jnp.float32(1.0), jnp.exp(jnp.minimum(pre, 0.0)))


def start_values(values_hbm, values, sems):
    copies = [
        pltpu.make_async_copy(
            values_hbm.at[pl.ds(c * CHUNK, CHUNK)], values.at[pl.ds(c * CHUNK, CHUNK)], sems.at[c]
        )
        for c in range(values.shape[0] // CHUNK)
    ]
    for copy in copies:
        copy.start()
    return copies


def walk(copies, live, step):
    for c, copy in enumerate(copies):
        copy.wait()
        left = jnp.clip(live - c * CHUNK, 0, CHUNK)

        def one(g, carry, c=c):
            step(c * CHUNK + g * GROUP)
            return carry

        lax.fori_loop(0, (left + GROUP - 1) // GROUP, one, 0)


def forward_kernel(rows, cols, live_ref, core_ref, values_hbm, src, kept, sent, values, acc, sems):
    live, core = live_ref[0], core_ref[0]
    copies = start_values(values_hbm, values, sems)
    half = kept.shape[0]
    acc[...] = jnp.zeros_like(acc)

    def slot(t):
        return (lax.rem(t, 2) ^ core) * half + ((t // 2) & 3) * 4 + t // 8

    def step(first):
        for u in range(GROUP):
            s = first + u
            dest = jnp.where(s < live, slot(rows[s]), 2 * half)
            acc[dest] += jnp.dot(values[s], src[cols[s]], preferred_element_type=jnp.float32)

    walk(copies, live, step)
    sent[...] = acc[half : 2 * half].astype(sent.dtype)
    kept[...] = acc[:half].astype(kept.dtype)


def backward_kernel(rows, cols, live_ref, place, weight_rows, values_hbm, *refs):
    blocks, (out, values, src, acc, sems, src_sems) = refs[:8], refs[8:]
    live = live_ref[0]
    core, x, y = place[0], place[1], place[2]
    depth = blocks[0].shape[0]
    fetch = [
        pltpu.make_async_copy(block, src.at[pl.ds(k * depth, depth)], src_sems.at[k]) for k, block in enumerate(blocks)
    ]
    for copy in fetch:
        copy.start()
    copies = start_values(values_hbm, values, sems)
    tiles, width = out.shape[0], out.shape[-1]
    side = values.shape[1]
    acc[...] = jnp.zeros_like(acc)
    for copy in fetch:
        copy.wait()

    def slot(t):
        return (lax.rem(t, 2) ^ core) * 16 + ((x - t // 2) & 3) * 4 + ((y - t // 8) & 3)

    bias = jnp.zeros((8, width), jnp.float32)
    for t in range(2 * tiles):
        block = src[slot(jnp.int32(t))].astype(jnp.float32)
        bias += jnp.sum(block.reshape(side // 8, 8, width), axis=0)
    bias = jnp.sum(bias, axis=0, keepdims=True)
    high = bias.astype(jnp.bfloat16).astype(jnp.float32)
    row = lax.broadcasted_iota(jnp.int32, (8, width), 0)
    tail = jnp.where(row == 0, high, jnp.where(row == 1, bias - high, 0.0)).astype(out.dtype)
    piece = weight_rows[...].astype(out.dtype)
    for t in range(tiles):
        out[t, side : side + 16, :] = piece
        out[t, side + 16 :, :] = tail

    def step(first):
        for u in range(GROUP):
            s = first + u
            dest = jnp.where(s < live, cols[s], tiles)
            acc[dest] += lax.dot_general(
                values[s], src[slot(rows[s])], (((0,), (0,)), ((), ())), preferred_element_type=jnp.float32
            )

    walk(copies, live, step)
    for t in range(tiles):
        out[t, :side, :] = acc[t].astype(out.dtype)


SMEM = pl.BlockSpec(memory_space=pltpu.SMEM)
VMEM = pl.BlockSpec(memory_space=pltpu.VMEM)
ANY = pl.BlockSpec(memory_space=pl.ANY)
HBM = pl.BlockSpec(memory_space=pltpu.HBM)


def cost(slots, side, width):
    return pl.CostEstimate(
        flops=2 * slots * side * side * width, bytes_accessed=2 * slots * side * side, transcendentals=0
    )


def spread_forward(rows, cols, live, place, values, src, row_tiles):
    slots, side, _ = values.shape
    width = src.shape[-1]
    half = jax.ShapeDtypeStruct((row_tiles // 2, side, width), jnp.bfloat16)
    return pl.pallas_call(
        forward_kernel,
        out_shape=(half, half),
        in_specs=[SMEM, SMEM, SMEM, SMEM, HBM, VMEM],
        out_specs=(VMEM, VMEM),
        scratch_shapes=[
            pltpu.VMEM((slots, side, side), jnp.bfloat16),
            pltpu.VMEM((row_tiles + 1, side, width), jnp.float32),
            pltpu.SemaphoreType.DMA((slots // CHUNK,)),
        ],
        compiler_params=pltpu.CompilerParams(vmem_limit_bytes=40 << 20),
        cost_estimate=cost(slots, side, width),
        name="forward_tiles",
    )(rows, cols, live, place, values, src)


def spread_backward(rows, cols, live, place, weight_rows, values, blocks, col_tiles):
    slots, side, _ = values.shape
    depth, _, width = blocks[0].shape
    return pl.pallas_call(
        backward_kernel,
        out_shape=jax.ShapeDtypeStruct((col_tiles, side + 24, width), jnp.bfloat16),
        in_specs=[SMEM, SMEM, SMEM, SMEM, VMEM, HBM] + [ANY] * len(blocks),
        out_specs=VMEM,
        scratch_shapes=[
            pltpu.VMEM((slots, side, side), jnp.bfloat16),
            pltpu.VMEM((len(blocks) * depth, side, width), jnp.bfloat16),
            pltpu.VMEM((col_tiles + 1, side, width), jnp.float32),
            pltpu.SemaphoreType.DMA((slots // CHUNK,)),
            pltpu.SemaphoreType.DMA((len(blocks),)),
        ],
        compiler_params=pltpu.CompilerParams(vmem_limit_bytes=40 << 20),
        cost_estimate=cost(slots, side, width),
        name="backward_tiles",
    )(rows, cols, live, place, weight_rows, values, *blocks)


def around(x, axis, size):
    return [x] + [lax.ppermute(x, axis, [(i, (i + k) % size) for i in range(size)]) for k in range(1, size)]


def swap(x):
    return lax.ppermute(x, "core", [(0, 1), (1, 0)])


def exchange(x, axes):
    return lax.all_to_all(x, axes, 0, 0, tiled=True)


def gather(x, axes, size):
    copies = lax.optimization_barrier(jnp.broadcast_to(x[None], (size,) + x.shape))
    return exchange(copies, axes)


def add_up(x):
    return jnp.sum(x.astype(jnp.float32), axis=0)


def body(features, weight, bias, grad_out, tile_rows, tile_cols, tile_counts, tile_values):
    values = pltpu.with_memory_space_constraint(tile_values[0, 0], pltpu.HBM)
    rows, cols, live = tile_rows[0, 0], tile_cols[0, 0], tile_counts[0]
    side, width = features.shape
    row_tiles, col_tiles = 32, 16
    bf16 = jnp.bfloat16
    place = jnp.stack([lax.axis_index(axis) for axis in ("core", "x", "yl")]).astype(jnp.int32)

    block = gather(features, ROW, col_tiles)
    kept, sent = spread_forward(rows, cols, live, place, values, block, row_tiles)
    by_core = (kept.astype(jnp.float32) + swap(sent).astype(jnp.float32)).astype(bf16)
    by_x = add_up(exchange(by_core.reshape(4, 4, side, width), "x")).astype(bf16)
    mean = add_up(exchange(by_x, "yl"))
    pre = (
        jnp.dot(mean, weight.astype(jnp.float32), precision=lax.Precision.HIGHEST, preferred_element_type=jnp.float32)
        + bias[None, :]
    )
    grad_pre = (grad_out.astype(jnp.float32) * elu_slope(pre)).astype(bf16)
    output = elu_value(pre).astype(bf16)

    grad32 = grad_pre.astype(jnp.float32)
    weight_term = lax.dot_general(
        mean, grad32, (((0,), (0,)), ((), ())), precision=lax.Precision.HIGHEST, preferred_element_type=jnp.float32
    )
    along_y = jnp.stack(around(grad_pre, "yl", 4))
    own = around(along_y, "x", 4)
    blocks = own + [swap(block) for block in own]

    pieces = exchange(weight_term.astype(bf16).reshape(16, width // 16, width), ROW)
    pieces, _ = lax.optimization_barrier((pieces, own[3]))
    weight_rows = add_up(gather(add_up(pieces).astype(bf16), COL, 32))
    back = exchange(spread_backward(rows, cols, live, place, weight_rows, values, blocks, col_tiles), ROW)
    grad_mixed = add_up(back[:, :side]).astype(bf16)
    grad_weight = back[:, side : side + 16].reshape(width, width).astype(jnp.float32)
    bias_rows = add_up(back[:, side + 16 :])
    grad_bias = bias_rows[0] + bias_rows[1]
    grad_features = lax.dot_general(
        grad_mixed, weight, (((1,), (1,)), ((), ())), preferred_element_type=jnp.float32
    ).astype(bf16)
    return (output, grad_features, grad_weight, grad_bias)


def solution(mesh):
    fine = Mesh(mesh.devices.reshape(2, 8, 4, 4, 2), ALL)
    placed = (
        P(COL + ROW, None),
        P(),
        P(),
        P(ALL, None),
        P(ROW, COL, None),
        P(ROW, COL, None),
        P(ROW, COL),
        P(ROW, COL, None, None, None),
    )
    return jax.shard_map(
        body,
        mesh=fine,
        in_specs=placed,
        out_specs=(P(ALL, None), P(COL + ROW, None), P(), P()),
        check_vma=False,
    )
```

```python
import jax
import jax.numpy as jnp
from jax import lax
from jax.experimental import pallas as pl
from jax.experimental.pallas import tpu as pltpu
from jax.sharding import Mesh
from jax.sharding import PartitionSpec as P

ROW = ("yh", "z")
COL = ("yl", "x", "core")
ALL = ROW + COL
CHUNK = 16
GROUP = 16


def elu_value(pre):
    return jnp.where(pre > 0, pre, jnp.expm1(jnp.minimum(pre, 0.0)))


def elu_slope(pre):
    return jnp.where(pre > 0, jnp.float32(1.0), jnp.exp(jnp.minimum(pre, 0.0)))


def start_values(values_hbm, values, sems):
    copies = [
        pltpu.make_async_copy(
            values_hbm.at[pl.ds(c * CHUNK, CHUNK)], values.at[pl.ds(c * CHUNK, CHUNK)], sems.at[c]
        )
        for c in range(values.shape[0] // CHUNK)
    ]
    for copy in copies:
        copy.start()
    return copies


def walk(copies, live, step):
    for c, copy in enumerate(copies):
        copy.wait()
        left = jnp.clip(live - c * CHUNK, 0, CHUNK)

        def one(g, carry, c=c):
            step(c * CHUNK + g * GROUP)
            return carry

        lax.fori_loop(0, (left + GROUP - 1) // GROUP, one, 0)


def forward_kernel(rows, cols, live_ref, core_ref, values_hbm, src, kept, sent, values, acc, sems):
    live, core = live_ref[0], core_ref[0]
    copies = start_values(values_hbm, values, sems)
    half = kept.shape[0]
    acc[...] = jnp.zeros_like(acc)

    def slot(t):
        return (lax.rem(t, 2) ^ core) * half + ((t // 2) & 3) * 4 + t // 8

    def step(first):
        for u in range(GROUP):
            s = first + u
            dest = jnp.where(s < live, slot(rows[s]), 2 * half)
            acc[dest] += jnp.dot(values[s], src[cols[s]], preferred_element_type=jnp.float32)

    walk(copies, live, step)
    sent[...] = acc[half : 2 * half].astype(sent.dtype)
    kept[...] = acc[:half].astype(kept.dtype)


def backward_kernel(rows, cols, live_ref, place, weight_rows, values_hbm, *refs):
    blocks, (out, values, src, acc, sems, src_sems) = refs[:8], refs[8:]
    live = live_ref[0]
    core, x, y = place[0], place[1], place[2]
    depth = blocks[0].shape[0]
    fetch = [
        pltpu.make_async_copy(block, src.at[pl.ds(k * depth, depth)], src_sems.at[k]) for k, block in enumerate(blocks)
    ]
    for copy in fetch:
        copy.start()
    copies = start_values(values_hbm, values, sems)
    tiles, width = out.shape[0], out.shape[-1]
    side = values.shape[1]
    acc[...] = jnp.zeros_like(acc)
    for copy in fetch:
        copy.wait()

    def slot(t):
        return (lax.rem(t, 2) ^ core) * 16 + ((x - t // 2) & 3) * 4 + ((y - t // 8) & 3)

    bias = jnp.zeros((8, width), jnp.float32)
    for t in range(2 * tiles):
        block = src[slot(jnp.int32(t))].astype(jnp.float32)
        bias += jnp.sum(block.reshape(side // 8, 8, width), axis=0)
    bias = jnp.sum(bias, axis=0, keepdims=True)
    high = bias.astype(jnp.bfloat16).astype(jnp.float32)
    row = lax.broadcasted_iota(jnp.int32, (8, width), 0)
    tail = jnp.where(row == 0, high, jnp.where(row == 1, bias - high, 0.0)).astype(out.dtype)
    piece = weight_rows[...].astype(out.dtype)
    for t in range(tiles):
        out[t, side : side + 16, :] = piece
        out[t, side + 16 :, :] = tail

    def step(first):
        for u in range(GROUP):
            s = first + u
            dest = jnp.where(s < live, cols[s], tiles)
            acc[dest] += lax.dot_general(
                values[s], src[slot(rows[s])], (((0,), (0,)), ((), ())), preferred_element_type=jnp.float32
            )

    walk(copies, live, step)
    for t in range(tiles):
        out[t, :side, :] = acc[t].astype(out.dtype)


SMEM = pl.BlockSpec(memory_space=pltpu.SMEM)
VMEM = pl.BlockSpec(memory_space=pltpu.VMEM)
ANY = pl.BlockSpec(memory_space=pl.ANY)
HBM = pl.BlockSpec(memory_space=pltpu.HBM)


def cost(slots, side, width):
    return pl.CostEstimate(
        flops=2 * slots * side * side * width, bytes_accessed=2 * slots * side * side, transcendentals=0
    )


def spread_forward(rows, cols, live, place, values, src, row_tiles):
    slots, side, _ = values.shape
    width = src.shape[-1]
    half = jax.ShapeDtypeStruct((row_tiles // 2, side, width), jnp.bfloat16)
    return pl.pallas_call(
        forward_kernel,
        out_shape=(half, half),
        in_specs=[SMEM, SMEM, SMEM, SMEM, HBM, VMEM],
        out_specs=(VMEM, VMEM),
        scratch_shapes=[
            pltpu.VMEM((slots, side, side), jnp.bfloat16),
            pltpu.VMEM((row_tiles + 1, side, width), jnp.float32),
            pltpu.SemaphoreType.DMA((slots // CHUNK,)),
        ],
        compiler_params=pltpu.CompilerParams(vmem_limit_bytes=40 << 20),
        cost_estimate=cost(slots, side, width),
        name="forward_tiles",
    )(rows, cols, live, place, values, src)


def spread_backward(rows, cols, live, place, weight_rows, values, blocks, col_tiles):
    slots, side, _ = values.shape
    depth, _, width = blocks[0].shape
    return pl.pallas_call(
        backward_kernel,
        out_shape=jax.ShapeDtypeStruct((col_tiles, side + 24, width), jnp.bfloat16),
        in_specs=[SMEM, SMEM, SMEM, SMEM, VMEM, HBM] + [ANY] * len(blocks),
        out_specs=VMEM,
        scratch_shapes=[
            pltpu.VMEM((slots, side, side), jnp.bfloat16),
            pltpu.VMEM((len(blocks) * depth, side, width), jnp.bfloat16),
            pltpu.VMEM((col_tiles + 1, side, width), jnp.float32),
            pltpu.SemaphoreType.DMA((slots // CHUNK,)),
            pltpu.SemaphoreType.DMA((len(blocks),)),
        ],
        compiler_params=pltpu.CompilerParams(vmem_limit_bytes=40 << 20),
        cost_estimate=cost(slots, side, width),
        name="backward_tiles",
    )(rows, cols, live, place, weight_rows, values, *blocks)


def around(x, axis, size):
    return [x] + [lax.ppermute(x, axis, [(i, (i + k) % size) for i in range(size)]) for k in range(1, size)]


def swap(x):
    return lax.ppermute(x, "core", [(0, 1), (1, 0)])


def exchange(x, axes):
    return lax.all_to_all(x, axes, 0, 0, tiled=True)


def gather(x, axes, size):
    copies = lax.optimization_barrier(jnp.broadcast_to(x[None], (size,) + x.shape))
    return exchange(copies, axes)


def add_up(x):
    return jnp.sum(x.astype(jnp.float32), axis=0)


def body(features, weight, bias, grad_out, tile_rows, tile_cols, tile_counts, tile_values):
    values = pltpu.with_memory_space_constraint(tile_values[0, 0], pltpu.HBM)
    rows, cols, live = tile_rows[0, 0], tile_cols[0, 0], tile_counts[0]
    side, width = features.shape
    row_tiles, col_tiles = 32, 16
    bf16 = jnp.bfloat16
    place = jnp.stack([lax.axis_index(axis) for axis in ("core", "x", "yl")]).astype(jnp.int32)

    block = gather(features, ROW, col_tiles)
    kept, sent = spread_forward(rows, cols, live, place, values, block, row_tiles)
    by_core = (kept.astype(jnp.float32) + swap(sent).astype(jnp.float32)).astype(bf16)
    by_x = add_up(exchange(by_core.reshape(4, 4, side, width), "x")).astype(bf16)
    mean = add_up(exchange(by_x, "yl"))
    pre = (
        jnp.dot(mean, weight.astype(jnp.float32), precision=lax.Precision.HIGHEST, preferred_element_type=jnp.float32)
        + bias[None, :]
    )
    grad_pre = (grad_out.astype(jnp.float32) * elu_slope(pre)).astype(bf16)
    output = elu_value(pre).astype(bf16)

    grad32 = grad_pre.astype(jnp.float32)
    weight_term = lax.dot_general(
        mean, grad32, (((0,), (0,)), ((), ())), precision=lax.Precision.HIGHEST, preferred_element_type=jnp.float32
    )
    along_y = jnp.stack(around(grad_pre, "yl", 4))
    own = around(along_y, "x", 4)
    blocks = own + [swap(block) for block in own]

    pieces = exchange(weight_term.astype(bf16).reshape(16, width // 16, width), ROW)
    pieces, _ = lax.optimization_barrier((pieces, along_y))
    weight_rows = add_up(gather(add_up(pieces).astype(bf16), COL, 32))
    back = exchange(spread_backward(rows, cols, live, place, weight_rows, values, blocks, col_tiles), ROW)
    grad_mixed = add_up(back[:, :side]).astype(bf16)
    grad_weight = back[:, side : side + 16].reshape(width, width).astype(jnp.float32)
    bias_rows = add_up(back[:, side + 16 :])
    grad_bias = bias_rows[0] + bias_rows[1]
    grad_features = lax.dot_general(
        grad_mixed, weight, (((1,), (1,)), ((), ())), preferred_element_type=jnp.float32
    ).astype(bf16)
    return (output, grad_features, grad_weight, grad_bias)


def solution(mesh):
    fine = Mesh(mesh.devices.reshape(2, 8, 4, 4, 2), ALL)
    placed = (
        P(COL + ROW, None),
        P(),
        P(),
        P(ALL, None),
        P(ROW, COL, None),
        P(ROW, COL, None),
        P(ROW, COL),
        P(ROW, COL, None, None, None),
    )
    return jax.shard_map(
        body,
        mesh=fine,
        in_specs=placed,
        out_specs=(P(ALL, None), P(COL + ROW, None), P(), P()),
        check_vma=False,
    )
```

```python
import jax
import jax.numpy as jnp
from jax import lax
from jax.experimental import pallas as pl
from jax.experimental.pallas import tpu as pltpu
from jax.sharding import Mesh
from jax.sharding import PartitionSpec as P

ROW = ("yh", "z")
COL = ("yl", "x", "core")
ALL = ROW + COL
GROUP = 32


def elu_value(pre):
    return jnp.where(pre > 0, pre, jnp.expm1(jnp.minimum(pre, 0.0)))


def elu_slope(pre):
    return jnp.where(pre > 0, jnp.float32(1.0), jnp.exp(jnp.minimum(pre, 0.0)))


def start_values(values_hbm, values, sems):
    copies = [
        pltpu.make_async_copy(
            values_hbm.at[pl.ds(c * GROUP, GROUP)], values.at[pl.ds(c * GROUP, GROUP)], sems.at[c]
        )
        for c in range(values.shape[0] // GROUP)
    ]
    for copy in copies:
        copy.start()
    return copies


def walk(live, step, copies=()):
    if not copies:

        def one(g, carry):
            step(g * GROUP)
            return carry

        lax.fori_loop(0, (live + GROUP - 1) // GROUP, one, 0)
    for c, copy in enumerate(copies):
        copy.wait()
        pl.when(c * GROUP < live)(lambda c=c: step(c * GROUP))


def forward_kernel(rows, cols, live_ref, core_ref, values_hbm, src, kept, sent, values, acc, sems):
    live, core = live_ref[0], core_ref[0]
    copies = start_values(values_hbm, values, sems)
    half = kept.shape[0]
    acc[...] = jnp.zeros_like(acc)

    def slot(t):
        return (lax.rem(t, 2) ^ core) * half + ((t // 2) & 3) * 4 + t // 8

    def step(first):
        for u in range(GROUP):
            s = first + u
            dest = jnp.where(s < live, slot(rows[s]), 2 * half)
            acc[dest] += jnp.dot(values[s], src[cols[s]], preferred_element_type=jnp.float32)

    walk(live, step, copies)
    sent[...] = acc[half : 2 * half].astype(sent.dtype)
    kept[...] = acc[:half].astype(kept.dtype)


def backward_kernel(rows, cols, live_ref, core_ref, values, own, other, out, src, acc, src_sems):
    live, core = live_ref[0], core_ref[0]
    fetch = [
        pltpu.make_async_copy(own, src.at[pl.ds(core * 4, 4)], src_sems.at[0]),
        pltpu.make_async_copy(other, src.at[pl.ds((1 - core) * 4, 4)], src_sems.at[1]),
    ]
    for copy in fetch:
        copy.start()
    tiles, side = out.shape[0], values.shape[1]
    gathered = 4 * side
    acc[...] = jnp.zeros_like(acc)
    for copy in fetch:
        copy.wait()

    terms = jnp.zeros((16, out.shape[-1]), jnp.float32)
    bias = jnp.zeros((8, out.shape[-1]), jnp.float32)
    for k in range(8):
        terms += src[k, gathered:, :].astype(jnp.float32)
        for part in range(0, gathered, side):
            block = src[k, part : part + side, :].astype(jnp.float32)
            bias += jnp.sum(block.reshape(side // 8, 8, -1), axis=0)
    bias = jnp.sum(bias, axis=0, keepdims=True)
    high = bias.astype(jnp.bfloat16).astype(jnp.float32)
    row = lax.broadcasted_iota(jnp.int32, (8, out.shape[-1]), 0)
    tail = jnp.where(row == 0, high, jnp.where(row == 1, bias - high, 0.0))
    mine = jnp.where(core == 0, terms[:8], terms[8:])
    tail = jnp.concatenate([mine, tail]).astype(out.dtype)
    for t in range(tiles):
        out[t, side:, :] = tail

    def step(first):
        for u in range(GROUP):
            s = first + u
            dest = jnp.where(s < live, cols[s], tiles)
            t = rows[s]
            block = src[lax.rem(t, 2) * 4 + ((t // 2) & 3), pl.ds(pl.multiple_of(t // 8 * side, side), side), :]
            acc[dest] += lax.dot_general(
                values[s], block, (((0,), (0,)), ((), ())), preferred_element_type=jnp.float32
            )

    walk(live, step)
    for t in range(tiles):
        out[t, :side, :] = acc[t].astype(out.dtype)


SMEM = pl.BlockSpec(memory_space=pltpu.SMEM)
VMEM = pl.BlockSpec(memory_space=pltpu.VMEM)
ANY = pl.BlockSpec(memory_space=pl.ANY)
HBM = pl.BlockSpec(memory_space=pltpu.HBM)


def cost(slots, side, width):
    return pl.CostEstimate(
        flops=2 * slots * side * side * width, bytes_accessed=2 * slots * side * side, transcendentals=0
    )


def spread_forward(rows, cols, live, core, values, src, row_tiles):
    slots, side, _ = values.shape
    width = src.shape[-1]
    half = jax.ShapeDtypeStruct((row_tiles // 2, side, width), jnp.bfloat16)
    return pl.pallas_call(
        forward_kernel,
        out_shape=(half, half),
        in_specs=[SMEM, SMEM, SMEM, SMEM, HBM, VMEM],
        out_specs=(VMEM, VMEM),
        scratch_shapes=[
            pltpu.VMEM((slots, side, side), jnp.bfloat16),
            pltpu.VMEM((row_tiles + 1, side, width), jnp.float32),
            pltpu.SemaphoreType.DMA((slots // GROUP,)),
        ],
        compiler_params=pltpu.CompilerParams(vmem_limit_bytes=40 << 20),
        cost_estimate=cost(slots, side, width),
        name="forward_tiles",
    )(rows, cols, live, core, values, src)


def spread_backward(rows, cols, live, core, values, own, other, col_tiles):
    slots, side, _ = values.shape
    width = own.shape[-1]
    return pl.pallas_call(
        backward_kernel,
        out_shape=jax.ShapeDtypeStruct((col_tiles, side + 16, width), jnp.bfloat16),
        in_specs=[SMEM, SMEM, SMEM, SMEM, VMEM, ANY, ANY],
        out_specs=VMEM,
        scratch_shapes=[
            pltpu.VMEM((2 * own.shape[0],) + own.shape[1:], jnp.bfloat16),
            pltpu.VMEM((col_tiles + 1, side, width), jnp.float32),
            pltpu.SemaphoreType.DMA((2,)),
        ],
        compiler_params=pltpu.CompilerParams(vmem_limit_bytes=32 << 20),
        cost_estimate=cost(slots, side, width),
        name="backward_tiles",
    )(rows, cols, live, core, values, own, other)


def swap(x):
    return lax.ppermute(x, "core", [(0, 1), (1, 0)])


def exchange(x, axes):
    return lax.all_to_all(x, axes, 0, 0, tiled=True)


def gather(x, axes, size):
    copies = lax.optimization_barrier(jnp.broadcast_to(x[None], (size,) + x.shape))
    return exchange(copies, axes)


def gather_and_scatter(x, pieces, axes):
    copies = jnp.broadcast_to(x[None], pieces.shape[:1] + x.shape)
    return exchange(lax.optimization_barrier(jnp.concatenate([copies, pieces], axis=1)), axes)


def add_up(x):
    return jnp.sum(x.astype(jnp.float32), axis=0)


def body(features, weight, bias, grad_out, tile_rows, tile_cols, tile_counts, tile_values):
    values = tile_values[0, 0]
    in_hbm = pltpu.with_memory_space_constraint(values, pltpu.HBM)
    rows, cols, live = tile_rows[0, 0], tile_cols[0, 0], tile_counts[0]
    side, width = features.shape
    row_tiles, col_tiles = 32, 16
    bf16 = jnp.bfloat16
    core = lax.axis_index("core").astype(jnp.int32).reshape(1)

    block = gather(features, ROW, col_tiles)
    kept, sent = spread_forward(rows, cols, live, core, in_hbm, block, row_tiles)
    by_core = (kept.astype(jnp.float32) + swap(sent).astype(jnp.float32)).astype(bf16)
    by_x = add_up(exchange(by_core.reshape(4, 4, side, width), "x")).astype(bf16)
    mean = add_up(exchange(by_x, "yl"))
    pre = (
        jnp.dot(mean, weight.astype(jnp.float32), precision=lax.Precision.HIGHEST, preferred_element_type=jnp.float32)
        + bias[None, :]
    )
    grad_pre = (grad_out.astype(jnp.float32) * elu_slope(pre)).astype(bf16)
    output = elu_value(pre).astype(bf16)

    grad32 = grad_pre.astype(jnp.float32)
    weight_term = lax.dot_general(
        mean, grad32, (((0,), (0,)), ((), ())), precision=lax.Precision.HIGHEST, preferred_element_type=jnp.float32
    )
    terms = weight_term.astype(bf16).reshape(4, width // 4, width)
    along_y = gather_and_scatter(grad_pre, terms, "yl")
    terms = add_up(along_y[:, side:]).astype(bf16).reshape(4, width // 16, width)
    own = gather_and_scatter(along_y[:, :side].reshape(4 * side, width), terms, "x")
    back = spread_backward(rows, cols, live, core, values, own, swap(own), col_tiles)

    reduced = add_up(exchange(back, ROW))
    grad_mixed = reduced[:side].astype(bf16)
    grad_weight = gather(reduced[side : side + 8], COL, 32).reshape(width, width)
    grad_bias = reduced[side + 8] + reduced[side + 9]
    grad_features = lax.dot_general(
        grad_mixed, weight, (((1,), (1,)), ((), ())), preferred_element_type=jnp.float32
    ).astype(bf16)
    return (output, grad_features, grad_weight, grad_bias)


def solution(mesh):
    fine = Mesh(mesh.devices.reshape(2, 8, 4, 4, 2), ALL)
    placed = (
        P(COL + ROW, None),
        P(),
        P(),
        P(ALL, None),
        P(ROW, COL, None),
        P(ROW, COL, None),
        P(ROW, COL),
        P(ROW, COL, None, None, None),
    )
    return jax.shard_map(
        body,
        mesh=fine,
        in_specs=placed,
        out_specs=(P(ALL, None), P(COL + ROW, None), P(), P()),
        check_vma=False,
    )
```

```python
import jax
import jax.numpy as jnp
from jax import lax
from jax.experimental import pallas as pl
from jax.experimental.pallas import tpu as pltpu
from jax.sharding import Mesh
from jax.sharding import PartitionSpec as P

ROW = ("yh", "z")
COL = ("yl", "x", "core")
ALL = ROW + COL
GROUP = 32


def elu_value(pre):
    return jnp.where(pre > 0, pre, jnp.expm1(jnp.minimum(pre, 0.0)))


def elu_slope(pre):
    return jnp.where(pre > 0, jnp.float32(1.0), jnp.exp(jnp.minimum(pre, 0.0)))


def start_values(values_hbm, values, sems):
    copies = [
        pltpu.make_async_copy(
            values_hbm.at[pl.ds(c * GROUP, GROUP)], values.at[pl.ds(c * GROUP, GROUP)], sems.at[c]
        )
        for c in range(values.shape[0] // GROUP)
    ]
    for copy in copies:
        copy.start()
    return copies


def walk(live, step, copies=()):
    if not copies:

        def one(g, carry):
            step(g * GROUP)
            return carry

        lax.fori_loop(0, (live + GROUP - 1) // GROUP, one, 0)
    for c, copy in enumerate(copies):
        copy.wait()
        pl.when(c * GROUP < live)(lambda c=c: step(c * GROUP))


def forward_kernel(rows, cols, live_ref, core_ref, values_hbm, src, kept, sent, values, acc, sems):
    live, core = live_ref[0], core_ref[0]
    copies = start_values(values_hbm, values, sems)
    half = kept.shape[0]
    acc[...] = jnp.zeros_like(acc)

    def slot(t):
        return (lax.rem(t, 2) ^ core) * half + ((t // 2) & 3) * 4 + t // 8

    def step(first):
        for u in range(GROUP):
            s = first + u
            dest = jnp.where(s < live, slot(rows[s]), 2 * half)
            acc[dest] += jnp.dot(values[s], src[cols[s]], preferred_element_type=jnp.float32)

    walk(live, step, copies)
    sent[...] = acc[half : 2 * half].astype(sent.dtype)
    kept[...] = acc[:half].astype(kept.dtype)


def backward_kernel(rows, cols, live_ref, core_ref, values, own, other, out, src, acc, src_sems):
    live, core = live_ref[0], core_ref[0]
    fetch = [
        pltpu.make_async_copy(own, src.at[pl.ds(core * 4, 4)], src_sems.at[0]),
        pltpu.make_async_copy(other, src.at[pl.ds((1 - core) * 4, 4)], src_sems.at[1]),
    ]
    for copy in fetch:
        copy.start()
    tiles, side = out.shape[0], values.shape[1]
    gathered = 4 * side
    acc[...] = jnp.zeros_like(acc)
    for copy in fetch:
        copy.wait()

    terms = jnp.zeros((16, out.shape[-1]), jnp.float32)
    bias = jnp.zeros((8, out.shape[-1]), jnp.float32)
    for k in range(8):
        terms += src[k, gathered:, :].astype(jnp.float32)
        for part in range(0, gathered, side):
            block = src[k, part : part + side, :].astype(jnp.float32)
            bias += jnp.sum(block.reshape(side // 8, 8, -1), axis=0)
    bias = jnp.sum(bias, axis=0, keepdims=True)
    high = bias.astype(jnp.bfloat16).astype(jnp.float32)
    row = lax.broadcasted_iota(jnp.int32, (8, out.shape[-1]), 0)
    tail = jnp.where(row == 0, high, jnp.where(row == 1, bias - high, 0.0))
    mine = jnp.where(core == 0, terms[:8], terms[8:])
    tail = jnp.concatenate([mine, tail]).astype(out.dtype)
    for t in range(tiles):
        out[t, side:, :] = tail

    def step(first):
        for u in range(GROUP):
            s = first + u
            dest = jnp.where(s < live, cols[s], tiles)
            t = rows[s]
            block = src[lax.rem(t, 2) * 4 + ((t // 2) & 3), pl.ds(pl.multiple_of(t // 8 * side, side), side), :]
            acc[dest] += lax.dot_general(
                values[s], block, (((0,), (0,)), ((), ())), preferred_element_type=jnp.float32
            )

    walk(live, step)
    for t in range(tiles):
        out[t, :side, :] = acc[t].astype(out.dtype)


SMEM = pl.BlockSpec(memory_space=pltpu.SMEM)
VMEM = pl.BlockSpec(memory_space=pltpu.VMEM)
ANY = pl.BlockSpec(memory_space=pl.ANY)
HBM = pl.BlockSpec(memory_space=pltpu.HBM)


def cost(slots, side, width):
    return pl.CostEstimate(
        flops=2 * slots * side * side * width, bytes_accessed=2 * slots * side * side, transcendentals=0
    )


def spread_forward(rows, cols, live, core, values, src, row_tiles):
    slots, side, _ = values.shape
    width = src.shape[-1]
    half = jax.ShapeDtypeStruct((row_tiles // 2, side, width), jnp.bfloat16)
    return pl.pallas_call(
        forward_kernel,
        out_shape=(half, half),
        in_specs=[SMEM, SMEM, SMEM, SMEM, HBM, VMEM],
        out_specs=(VMEM, VMEM),
        scratch_shapes=[
            pltpu.VMEM((slots, side, side), jnp.bfloat16),
            pltpu.VMEM((row_tiles + 1, side, width), jnp.float32),
            pltpu.SemaphoreType.DMA((slots // GROUP,)),
        ],
        compiler_params=pltpu.CompilerParams(vmem_limit_bytes=40 << 20),
        cost_estimate=cost(slots, side, width),
        name="forward_tiles",
    )(rows, cols, live, core, values, src)


def spread_backward(rows, cols, live, core, values, own, other, col_tiles):
    slots, side, _ = values.shape
    width = own.shape[-1]
    return pl.pallas_call(
        backward_kernel,
        out_shape=jax.ShapeDtypeStruct((col_tiles, side + 16, width), jnp.bfloat16),
        in_specs=[SMEM, SMEM, SMEM, SMEM, VMEM, ANY, ANY],
        out_specs=VMEM,
        scratch_shapes=[
            pltpu.VMEM((2 * own.shape[0],) + own.shape[1:], jnp.bfloat16),
            pltpu.VMEM((col_tiles + 1, side, width), jnp.float32),
            pltpu.SemaphoreType.DMA((2,)),
        ],
        compiler_params=pltpu.CompilerParams(vmem_limit_bytes=32 << 20),
        cost_estimate=cost(slots, side, width),
        name="backward_tiles",
    )(rows, cols, live, core, values, own, other)


def swap(x):
    return lax.ppermute(x, "core", [(0, 1), (1, 0)])


def exchange(x, axes):
    return lax.all_to_all(x, axes, 0, 0, tiled=True)


def gather(x, axes, size):
    copies = lax.optimization_barrier(jnp.broadcast_to(x[None], (size,) + x.shape))
    return exchange(copies, axes)


def gather_and_scatter(x, pieces, axes):
    copies = jnp.broadcast_to(x[None], pieces.shape[:1] + x.shape)
    return exchange(lax.optimization_barrier(jnp.concatenate([copies, pieces], axis=1)), axes)


def add_up(x):
    return jnp.sum(x.astype(jnp.float32), axis=0)


def body(features, weight, bias, grad_out, tile_rows, tile_cols, tile_counts, tile_values):
    values = tile_values[0, 0]
    in_hbm = pltpu.with_memory_space_constraint(values, pltpu.HBM)
    rows, cols, live = tile_rows[0, 0], tile_cols[0, 0], tile_counts[0]
    side, width = features.shape
    row_tiles, col_tiles = 32, 16
    bf16 = jnp.bfloat16
    core = lax.axis_index("core").astype(jnp.int32).reshape(1)

    block = gather(features, ROW, col_tiles)
    kept, sent = spread_forward(rows, cols, live, core, in_hbm, block, row_tiles)
    by_core = (kept.astype(jnp.float32) + swap(sent).astype(jnp.float32)).astype(bf16)
    by_x = add_up(exchange(by_core.reshape(4, 4, side, width), "x")).astype(bf16)
    mean = add_up(exchange(by_x, "yl"))
    pre = (
        jnp.dot(mean, weight.astype(jnp.float32), precision=lax.Precision.HIGHEST, preferred_element_type=jnp.float32)
        + bias[None, :]
    )
    grad_pre = (grad_out.astype(jnp.float32) * elu_slope(pre)).astype(bf16)
    output = elu_value(pre).astype(bf16)

    grad32 = grad_pre.astype(jnp.float32)
    weight_term = lax.dot_general(
        mean, grad32, (((0,), (0,)), ((), ())), precision=lax.Precision.HIGHEST, preferred_element_type=jnp.float32
    )
    terms = weight_term.astype(bf16).reshape(4, width // 4, width)
    along_y = gather_and_scatter(grad_pre, terms, "yl")
    terms = add_up(along_y[:, side:]).astype(bf16).reshape(4, width // 16, width)
    own = gather_and_scatter(along_y[:, :side].reshape(4 * side, width), terms, "x")
    back = spread_backward(rows, cols, live, core, values, own, swap(own), col_tiles)

    reduced = add_up(exchange(back, ROW))
    grad_mixed = reduced[:side].astype(bf16)
    grad_weight = gather(reduced[side : side + 8].astype(bf16), COL, 32).reshape(width, width).astype(jnp.float32)
    grad_bias = reduced[side + 8] + reduced[side + 9]
    grad_features = lax.dot_general(
        grad_mixed, weight, (((1,), (1,)), ((), ())), preferred_element_type=jnp.float32
    ).astype(bf16)
    return (output, grad_features, grad_weight, grad_bias)


def solution(mesh):
    fine = Mesh(mesh.devices.reshape(2, 8, 4, 4, 2), ALL)
    placed = (
        P(COL + ROW, None),
        P(),
        P(),
        P(ALL, None),
        P(ROW, COL, None),
        P(ROW, COL, None),
        P(ROW, COL),
        P(ROW, COL, None, None, None),
    )
    return jax.shard_map(
        body,
        mesh=fine,
        in_specs=placed,
        out_specs=(P(ALL, None), P(COL + ROW, None), P(), P()),
        check_vma=False,
    )
```

```python
import jax
import jax.numpy as jnp
from jax import lax
from jax.experimental import pallas as pl
from jax.experimental.pallas import tpu as pltpu
from jax.sharding import Mesh
from jax.sharding import PartitionSpec as P

ROW = ("yh", "z")
COL = ("yl", "x", "core")
PAIRS = ("z", "yh")
ALL = ROW + COL
GROUP = 32


def elu_value(pre):
    return jnp.where(pre > 0, pre, jnp.expm1(jnp.minimum(pre, 0.0)))


def elu_slope(pre):
    return jnp.where(pre > 0, jnp.float32(1.0), jnp.exp(jnp.minimum(pre, 0.0)))


def pair_slot(t):
    return (t & 7) * 2 + t // 8


def start_values(values_hbm, values, sems):
    copies = [
        pltpu.make_async_copy(
            values_hbm.at[pl.ds(c * GROUP, GROUP)], values.at[pl.ds(c * GROUP, GROUP)], sems.at[c]
        )
        for c in range(values.shape[0] // GROUP)
    ]
    for copy in copies:
        copy.start()
    return copies


def walk(live, step, copies=()):
    if not copies:

        def one(g, carry):
            step(g * GROUP)
            return carry

        lax.fori_loop(0, (live + GROUP - 1) // GROUP, one, 0)
    for c, copy in enumerate(copies):
        copy.wait()
        pl.when(c * GROUP < live)(lambda c=c: step(c * GROUP))


def forward_kernel(rows, cols, live_ref, core_ref, values_hbm, src, kept, sent, values, acc, sems):
    live, core = live_ref[0], core_ref[0]
    copies = start_values(values_hbm, values, sems)
    half = kept.shape[0]
    acc[...] = jnp.zeros_like(acc)

    def slot(t):
        return (lax.rem(t, 2) ^ core) * half + ((t // 2) & 3) * 4 + t // 8

    def step(first):
        for u in range(GROUP):
            s = first + u
            dest = jnp.where(s < live, slot(rows[s]), 2 * half)
            acc[dest] += jnp.dot(values[s], src[pair_slot(cols[s])], preferred_element_type=jnp.float32)

    walk(live, step, copies)
    sent[...] = acc[half : 2 * half].astype(sent.dtype)
    kept[...] = acc[:half].astype(kept.dtype)


def backward_kernel(rows, cols, live_ref, core_ref, values, own, other, out, src, acc, src_sems):
    live, core = live_ref[0], core_ref[0]
    fetch = [
        pltpu.make_async_copy(own, src.at[pl.ds(core * 4, 4)], src_sems.at[0]),
        pltpu.make_async_copy(other, src.at[pl.ds((1 - core) * 4, 4)], src_sems.at[1]),
    ]
    for copy in fetch:
        copy.start()
    tiles, side = out.shape[0], values.shape[1]
    gathered = 4 * side
    acc[...] = jnp.zeros_like(acc)
    for copy in fetch:
        copy.wait()

    terms = jnp.zeros((16, out.shape[-1]), jnp.float32)
    bias = jnp.zeros((8, out.shape[-1]), jnp.float32)
    for k in range(8):
        terms += src[k, gathered:, :].astype(jnp.float32)
        for part in range(0, gathered, side):
            block = src[k, part : part + side, :].astype(jnp.float32)
            bias += jnp.sum(block.reshape(side // 8, 8, -1), axis=0)
    bias = jnp.sum(bias, axis=0, keepdims=True)
    high = bias.astype(jnp.bfloat16).astype(jnp.float32)
    row = lax.broadcasted_iota(jnp.int32, (8, out.shape[-1]), 0)
    tail = jnp.where(row == 0, high, jnp.where(row == 1, bias - high, 0.0))
    mine = jnp.where(core == 0, terms[:8], terms[8:])
    tail = jnp.concatenate([mine, tail]).astype(out.dtype)
    for t in range(tiles):
        out[t, side:, :] = tail

    def step(first):
        for u in range(GROUP):
            s = first + u
            dest = jnp.where(s < live, pair_slot(cols[s]), tiles)
            t = rows[s]
            block = src[lax.rem(t, 2) * 4 + ((t // 2) & 3), pl.ds(pl.multiple_of(t // 8 * side, side), side), :]
            acc[dest] += lax.dot_general(
                values[s], block, (((0,), (0,)), ((), ())), preferred_element_type=jnp.float32
            )

    walk(live, step)
    for t in range(tiles):
        out[t, :side, :] = acc[t].astype(out.dtype)


SMEM = pl.BlockSpec(memory_space=pltpu.SMEM)
VMEM = pl.BlockSpec(memory_space=pltpu.VMEM)
ANY = pl.BlockSpec(memory_space=pl.ANY)
HBM = pl.BlockSpec(memory_space=pltpu.HBM)


def cost(slots, side, width):
    return pl.CostEstimate(
        flops=2 * slots * side * side * width, bytes_accessed=2 * slots * side * side, transcendentals=0
    )


def spread_forward(rows, cols, live, core, values, src, row_tiles):
    slots, side, _ = values.shape
    width = src.shape[-1]
    half = jax.ShapeDtypeStruct((row_tiles // 2, side, width), jnp.bfloat16)
    return pl.pallas_call(
        forward_kernel,
        out_shape=(half, half),
        in_specs=[SMEM, SMEM, SMEM, SMEM, HBM, VMEM],
        out_specs=(VMEM, VMEM),
        scratch_shapes=[
            pltpu.VMEM((slots, side, side), jnp.bfloat16),
            pltpu.VMEM((row_tiles + 1, side, width), jnp.float32),
            pltpu.SemaphoreType.DMA((slots // GROUP,)),
        ],
        compiler_params=pltpu.CompilerParams(vmem_limit_bytes=40 << 20),
        cost_estimate=cost(slots, side, width),
        name="forward_tiles",
    )(rows, cols, live, core, values, src)


def spread_backward(rows, cols, live, core, values, own, other, col_tiles):
    slots, side, _ = values.shape
    width = own.shape[-1]
    return pl.pallas_call(
        backward_kernel,
        out_shape=jax.ShapeDtypeStruct((col_tiles, side + 16, width), jnp.bfloat16),
        in_specs=[SMEM, SMEM, SMEM, SMEM, VMEM, ANY, ANY],
        out_specs=VMEM,
        scratch_shapes=[
            pltpu.VMEM((2 * own.shape[0],) + own.shape[1:], jnp.bfloat16),
            pltpu.VMEM((col_tiles + 1, side, width), jnp.float32),
            pltpu.SemaphoreType.DMA((2,)),
        ],
        compiler_params=pltpu.CompilerParams(vmem_limit_bytes=32 << 20),
        cost_estimate=cost(slots, side, width),
        name="backward_tiles",
    )(rows, cols, live, core, values, own, other)


def swap(x):
    return lax.ppermute(x, "core", [(0, 1), (1, 0)])


def exchange(x, axes):
    return lax.all_to_all(x, axes, 0, 0, tiled=True)


def gather(x, axes, size):
    copies = lax.optimization_barrier(jnp.broadcast_to(x[None], (size,) + x.shape))
    return exchange(copies, axes)


def gather_and_scatter(x, pieces, axes):
    copies = jnp.broadcast_to(x[None], pieces.shape[:1] + x.shape)
    return exchange(lax.optimization_barrier(jnp.concatenate([copies, pieces], axis=1)), axes)


def add_up(x):
    return jnp.sum(x.astype(jnp.float32), axis=0)


def body(features, weight, bias, grad_out, tile_rows, tile_cols, tile_counts, tile_values):
    values = tile_values[0, 0]
    in_hbm = pltpu.with_memory_space_constraint(values, pltpu.HBM)
    rows, cols, live = tile_rows[0, 0], tile_cols[0, 0], tile_counts[0]
    side, width = features.shape
    row_tiles, col_tiles = 32, 16
    bf16 = jnp.bfloat16
    core = lax.axis_index("core").astype(jnp.int32).reshape(1)

    block = gather(features, PAIRS, col_tiles)
    kept, sent = spread_forward(rows, cols, live, core, in_hbm, block, row_tiles)
    by_core = (kept.astype(jnp.float32) + swap(sent).astype(jnp.float32)).astype(bf16)
    by_x = add_up(exchange(by_core.reshape(4, 4, side, width), "x")).astype(bf16)
    mean = add_up(exchange(by_x, "yl"))
    pre = (
        jnp.dot(mean, weight.astype(jnp.float32), precision=lax.Precision.HIGHEST, preferred_element_type=jnp.float32)
        + bias[None, :]
    )
    grad_pre = (grad_out.astype(jnp.float32) * elu_slope(pre)).astype(bf16)
    output = elu_value(pre).astype(bf16)

    grad32 = grad_pre.astype(jnp.float32)
    weight_term = lax.dot_general(
        mean, grad32, (((0,), (0,)), ((), ())), precision=lax.Precision.HIGHEST, preferred_element_type=jnp.float32
    )
    terms = weight_term.astype(bf16).reshape(4, width // 4, width)
    along_y = gather_and_scatter(grad_pre, terms, "yl")
    terms = add_up(along_y[:, side:]).astype(bf16).reshape(4, width // 16, width)
    own = gather_and_scatter(along_y[:, :side].reshape(4 * side, width), terms, "x")
    back = spread_backward(rows, cols, live, core, values, own, swap(own), col_tiles)

    reduced = add_up(exchange(back, PAIRS))
    grad_mixed = reduced[:side].astype(bf16)
    grad_weight = gather(reduced[side : side + 8].astype(bf16), COL, 32).reshape(width, width).astype(jnp.float32)
    grad_bias = reduced[side + 8] + reduced[side + 9]
    grad_features = lax.dot_general(
        grad_mixed, weight, (((1,), (1,)), ((), ())), preferred_element_type=jnp.float32
    ).astype(bf16)
    return (output, grad_features, grad_weight, grad_bias)


def solution(mesh):
    fine = Mesh(mesh.devices.reshape(2, 8, 4, 4, 2), ALL)
    placed = (
        P(COL + ROW, None),
        P(),
        P(),
        P(ALL, None),
        P(ROW, COL, None),
        P(ROW, COL, None),
        P(ROW, COL),
        P(ROW, COL, None, None, None),
    )
    return jax.shard_map(
        body,
        mesh=fine,
        in_specs=placed,
        out_specs=(P(ALL, None), P(COL + ROW, None), P(), P()),
        check_vma=False,
    )
```

```python
import jax
import jax.numpy as jnp
from jax import lax
from jax.experimental import pallas as pl
from jax.experimental.pallas import tpu as pltpu
from jax.sharding import Mesh
from jax.sharding import PartitionSpec as P

ROW = ("yh", "z")
COL = ("yl", "x", "core")
ALL = ROW + COL
GROUP = 32


def elu_value(pre):
    return jnp.where(pre > 0, pre, jnp.expm1(jnp.minimum(pre, 0.0)))


def elu_slope(pre):
    return jnp.where(pre > 0, jnp.float32(1.0), jnp.exp(jnp.minimum(pre, 0.0)))


def start_values(values_hbm, values, sems):
    copies = [
        pltpu.make_async_copy(
            values_hbm.at[pl.ds(c * GROUP, GROUP)], values.at[pl.ds(c * GROUP, GROUP)], sems.at[c]
        )
        for c in range(values.shape[0] // GROUP)
    ]
    for copy in copies:
        copy.start()
    return copies


def walk(live, step, copies=()):
    if not copies:

        def one(g, carry):
            step(g * GROUP)
            return carry

        lax.fori_loop(0, (live + GROUP - 1) // GROUP, one, 0)
    for c, copy in enumerate(copies):
        copy.wait()
        pl.when(c * GROUP < live)(lambda c=c: step(c * GROUP))


def forward_kernel(rows, cols, live_ref, core_ref, values_hbm, src, kept, sent, values, acc, sems):
    live, core = live_ref[0], core_ref[0]
    copies = start_values(values_hbm, values, sems)
    half = kept.shape[0]
    acc[...] = jnp.zeros_like(acc)

    def slot(t):
        return (lax.rem(t, 2) ^ core) * half + ((t // 2) & 3) * 4 + t // 8

    def step(first):
        for u in range(GROUP):
            s = first + u
            dest = jnp.where(s < live, slot(rows[s]), 2 * half)
            acc[dest] += jnp.dot(values[s], src[cols[s]], preferred_element_type=jnp.float32)

    walk(live, step, copies)
    sent[...] = acc[half : 2 * half].astype(sent.dtype)
    kept[...] = acc[:half].astype(kept.dtype)


def backward_kernel(rows, cols, live_ref, core_ref, values, own, other, out, src, acc, src_sems):
    live, core = live_ref[0], core_ref[0]
    fetch = [
        pltpu.make_async_copy(own, src.at[pl.ds(core * 4, 4)], src_sems.at[0]),
        pltpu.make_async_copy(other, src.at[pl.ds((1 - core) * 4, 4)], src_sems.at[1]),
    ]
    for copy in fetch:
        copy.start()
    tiles, side = out.shape[0], values.shape[1]
    gathered = 4 * side
    acc[...] = jnp.zeros_like(acc)
    for copy in fetch:
        copy.wait()

    terms = jnp.zeros((16, out.shape[-1]), jnp.float32)
    bias = jnp.zeros((8, out.shape[-1]), jnp.float32)
    for k in range(8):
        terms += src[k, gathered:, :].astype(jnp.float32)
        for part in range(0, gathered, side):
            block = src[k, part : part + side, :].astype(jnp.float32)
            bias += jnp.sum(block.reshape(side // 8, 8, -1), axis=0)
    bias = jnp.sum(bias, axis=0, keepdims=True)
    high = bias.astype(jnp.bfloat16).astype(jnp.float32)
    row = lax.broadcasted_iota(jnp.int32, (8, out.shape[-1]), 0)
    tail = jnp.where(row == 0, high, jnp.where(row == 1, bias - high, 0.0))
    mine = jnp.where(core == 0, terms[:8], terms[8:])
    tail = jnp.concatenate([mine, tail]).astype(out.dtype)
    for t in range(tiles):
        out[t, side:, :] = tail

    def step(first):
        for u in range(GROUP):
            s = first + u
            dest = jnp.where(s < live, cols[s], tiles)
            t = rows[s]
            block = src[lax.rem(t, 2) * 4 + ((t // 2) & 3), pl.ds(pl.multiple_of(t // 8 * side, side), side), :]
            acc[dest] += lax.dot_general(
                values[s], block, (((0,), (0,)), ((), ())), preferred_element_type=jnp.float32
            )

    walk(live, step)
    for t in range(tiles):
        out[t, :side, :] = acc[t].astype(out.dtype)


SMEM = pl.BlockSpec(memory_space=pltpu.SMEM)
VMEM = pl.BlockSpec(memory_space=pltpu.VMEM)
ANY = pl.BlockSpec(memory_space=pl.ANY)
HBM = pl.BlockSpec(memory_space=pltpu.HBM)


def cost(slots, side, width):
    return pl.CostEstimate(
        flops=2 * slots * side * side * width, bytes_accessed=2 * slots * side * side, transcendentals=0
    )


def spread_forward(rows, cols, live, core, values, src, row_tiles):
    slots, side, _ = values.shape
    width = src.shape[-1]
    half = jax.ShapeDtypeStruct((row_tiles // 2, side, width), jnp.bfloat16)
    return pl.pallas_call(
        forward_kernel,
        out_shape=(half, half),
        in_specs=[SMEM, SMEM, SMEM, SMEM, HBM, VMEM],
        out_specs=(VMEM, VMEM),
        scratch_shapes=[
            pltpu.VMEM((slots, side, side), jnp.bfloat16),
            pltpu.VMEM((row_tiles + 1, side, width), jnp.float32),
            pltpu.SemaphoreType.DMA((slots // GROUP,)),
        ],
        compiler_params=pltpu.CompilerParams(vmem_limit_bytes=40 << 20),
        cost_estimate=cost(slots, side, width),
        name="forward_tiles",
    )(rows, cols, live, core, values, src)


def spread_backward(rows, cols, live, core, values, own, other, col_tiles):
    slots, side, _ = values.shape
    width = own.shape[-1]
    return pl.pallas_call(
        backward_kernel,
        out_shape=jax.ShapeDtypeStruct((col_tiles, side + 16, width), jnp.bfloat16),
        in_specs=[SMEM, SMEM, SMEM, SMEM, VMEM, ANY, ANY],
        out_specs=VMEM,
        scratch_shapes=[
            pltpu.VMEM((2 * own.shape[0],) + own.shape[1:], jnp.bfloat16),
            pltpu.VMEM((col_tiles + 1, side, width), jnp.float32),
            pltpu.SemaphoreType.DMA((2,)),
        ],
        compiler_params=pltpu.CompilerParams(vmem_limit_bytes=32 << 20),
        cost_estimate=cost(slots, side, width),
        name="backward_tiles",
    )(rows, cols, live, core, values, own, other)


def swap(x):
    return lax.ppermute(x, "core", [(0, 1), (1, 0)])


def exchange(x, axes):
    return lax.all_to_all(x, axes, 0, 0, tiled=True)


def gather(x, axes, size):
    copies = lax.optimization_barrier(jnp.broadcast_to(x[None], (size,) + x.shape))
    return exchange(copies, axes)


def gather_and_scatter(x, pieces, axes):
    copies = jnp.broadcast_to(x[None], pieces.shape[:1] + x.shape)
    return exchange(lax.optimization_barrier(jnp.concatenate([copies, pieces], axis=1)), axes)


def add_up(x):
    return jnp.sum(x.astype(jnp.float32), axis=0)


def body(features, weight, bias, grad_out, tile_rows, tile_cols, tile_counts, tile_values):
    values = tile_values[0, 0]
    in_hbm = pltpu.with_memory_space_constraint(values, pltpu.HBM)
    rows, cols, live = tile_rows[0, 0], tile_cols[0, 0], tile_counts[0]
    side, width = features.shape
    row_tiles, col_tiles = 32, 16
    bf16 = jnp.bfloat16
    core = lax.axis_index("core").astype(jnp.int32).reshape(1)

    block = gather(features, ROW, col_tiles)
    kept, sent = spread_forward(rows, cols, live, core, in_hbm, block, row_tiles)
    by_core = (kept.astype(jnp.float32) + swap(sent).astype(jnp.float32)).astype(bf16)
    by_x = add_up(exchange(by_core.reshape(4, 4, side, width), "x")).astype(bf16)
    mean = add_up(exchange(by_x, "yl"))
    pre = (
        jnp.dot(mean, weight.astype(jnp.float32), precision=lax.Precision.HIGHEST, preferred_element_type=jnp.float32)
        + bias[None, :]
    )
    grad_pre = (grad_out.astype(jnp.float32) * elu_slope(pre)).astype(bf16)

    grad32 = grad_pre.astype(jnp.float32)
    weight_term = lax.dot_general(
        mean, grad32, (((0,), (0,)), ((), ())), precision=lax.Precision.HIGHEST, preferred_element_type=jnp.float32
    )
    terms = weight_term.astype(bf16).reshape(4, width // 4, width)
    along_y = gather_and_scatter(grad_pre, terms, "yl")
    terms = add_up(along_y[:, side:]).astype(bf16).reshape(4, width // 16, width)
    own = gather_and_scatter(along_y[:, :side].reshape(4 * side, width), terms, "x")
    back = spread_backward(rows, cols, live, core, values, own, swap(own), col_tiles)

    late, back = lax.optimization_barrier((pre, back))
    output = elu_value(late).astype(bf16)
    reduced = add_up(exchange(back, ROW))
    grad_mixed = reduced[:side].astype(bf16)
    grad_weight = gather(reduced[side : side + 8].astype(bf16), COL, 32).reshape(width, width).astype(jnp.float32)
    grad_bias = reduced[side + 8] + reduced[side + 9]
    grad_features = lax.dot_general(
        grad_mixed, weight, (((1,), (1,)), ((), ())), preferred_element_type=jnp.float32
    ).astype(bf16)
    return (output, grad_features, grad_weight, grad_bias)


def solution(mesh):
    fine = Mesh(mesh.devices.reshape(2, 8, 4, 4, 2), ALL)
    placed = (
        P(COL + ROW, None),
        P(),
        P(),
        P(ALL, None),
        P(ROW, COL, None),
        P(ROW, COL, None),
        P(ROW, COL),
        P(ROW, COL, None, None, None),
    )
    return jax.shard_map(
        body,
        mesh=fine,
        in_specs=placed,
        out_specs=(P(ALL, None), P(COL + ROW, None), P(), P()),
        check_vma=False,
    )
```
